128 devices in a mesh: gx: 8 (over y_lo, x), gy: 16 (over z, y_hi, core).
Axes of the slice: x: 4, y: 4 (y_hi: 2, y_lo: 2; y = y_hi * 2 + y_lo), z: 4, core: 2. Of those that a mesh axis runs over, the one named last changes fastest.
Arguments:
- white_noise: float32 [8, 4096, 4096], P('gx', 'gy'), may hold values from -6 to 6
- amplitude: float32 [4096, 4096], P(None, 'gy'), may hold values from 0.24 to 1.26, as said below
- offsets: int32 [2], replicated, may hold values from 0 to 7
Outputs:
- trans_x: float32 [8, 4096, 4096], P('gx', 'gy')
- trans_y: float32 [8, 4096, 4096], P('gx', 'gy')
- upscaled: float32 [512, 512], P('gy', 'gx')
The draws below stay inside these ranges and needn't reach their ends.
Inputs may be any that keep to these rules, and one draw needn't show every extreme that they name: amplitude[ky, kx] equals amplitude[(4096 - ky) mod 4096, kx] and amplitude[ky, (4096 - kx) mod 4096]. offsets[0] shifts the coarse blocks along y, offsets[1] along x.
All inputs are finite; a program needn't handle non-finite values.
Results may differ from the reference program's by a relative error of at most 0.000096.
Values sent between devices are 32-bit elements; how exact they have to be, the bound alone decides.
A program may use at most 128 MiB of HBM per device.

```python
import math
import jax
import jax.numpy as jnp
from jax import lax

NX = 4096
NY = 4096
NZW = 8


def draw_amplitude(key, part):
    base_key = jax.random.fold_in(key, 11)
    table_shape = (NY // 2 + 1, NX // 2 + 1)
    base_table = jnp.exp(jax.random.uniform(base_key, table_shape, jnp.float32, math.log(0.25), math.log(1.25)))
    row_index = jnp.arange(NY, dtype=jnp.int32)
    column_index = jnp.arange(NX, dtype=jnp.int32)
    fold_y = jnp.minimum(row_index, NY - row_index)
    fold_x = jnp.minimum(column_index, NX - column_index)
    return base_table[fold_y[:, None], fold_x[None, :]].astype(jnp.float32)


def level_of(stream_key, extent, shards, smallest, top_value):
    def one(position, parts):
        draws = jax.random.uniform(jax.random.fold_in(jax.random.fold_in(stream_key, 6), position), (parts,), jnp.float32, smallest / len(shards), top_value / len(shards))
        return jnp.repeat(jnp.exp(draws), extent[position] // parts).reshape((-1,) + (1,) * (len(extent) - position - 1))

    gain = one(*shards[0])
    for cut in shards[1:]:
        gain = gain * one(*cut)
    return gain


def noise(stream_key, shape, deviation, reach, shards=(), kind=jnp.bfloat16):
    result = jax.random.normal(stream_key, shape, jnp.float32) * deviation
    if len(shards) > 0:
        result = level_of(stream_key, shape, shards, -0.22, 0.18) * result
    return jnp.clip(result, min=-reach, max=reach).astype(kind)


def setup_inputs(seed: int = 0) -> dict:
    splits = jax.random.split(jax.random.key(seed), 4)
    return {
        "white_noise": noise(splits[0], (NZW, NY, NX), 1.0, 6.0, ((0, 8), (1, 16)), jnp.float32),
        "amplitude": draw_amplitude(jax.random.fold_in(splits[3], 71), 0),
        "offsets": jax.random.randint(splits[2], (2,), 0, 8).astype(jnp.int32),
    }


def realize(one_layer, amplitude):
    spectrum = jnp.fft.fft2(one_layer)
    return jnp.real(jnp.fft.ifft2(spectrum * amplitude)).astype(jnp.float32)

def harmonic(first_cell, second_cell):
    return 2.0 * first_cell * second_cell / (first_cell + second_cell)

def reference(white_noise, amplitude, offsets):
    log_field = lax.map(lambda one_layer: realize(one_layer, amplitude), white_noise)
    permeability = jnp.exp(log_field)
    trans_x = harmonic(permeability, jnp.roll(permeability, -1, axis=2))
    trans_y = harmonic(permeability, jnp.roll(permeability, -1, axis=1))
    column_sums = jnp.stack([lax.optimization_barrier(jnp.sum(permeability, axis=0)), lax.optimization_barrier(jnp.sum(1.0 / permeability, axis=0))])
    shifted = jnp.roll(column_sums, -offsets[0], axis=1)
    shifted = jnp.roll(shifted, -offsets[1], axis=2)
    block_sums = shifted.reshape(2, NY // 8, 8, NX // 8, 8).sum(axis=(2, 4))
    upscaled = jnp.sqrt(block_sums[0] / block_sums[1])
    return (trans_x, trans_y, upscaled)
```

```python
import functools
import math

import jax
import jax.numpy as jnp
import numpy as np
from jax import lax
from jax.experimental import pallas as pl
from jax.experimental.pallas import tpu as pltpu
from jax.sharding import PartitionSpec as P

MESH = pl.DeviceIdType.MESH
F32 = jnp.float32
BF16 = jnp.bfloat16
L = 128
T = 32
N = L * T
SLOTS = 16
PER = 4
CHUNKS = SLOTS // PER
G = 16
GX = 8
ROWS = N // G


def _split_table(m):
    hi = m.astype(jnp.bfloat16)
    lo = (m - hi.astype(np.float64)).astype(jnp.bfloat16)
    return np.stack([np.asarray(hi), np.asarray(lo)])


def tables():
    l = np.arange(L)[:, None]
    k = np.arange(L)[None, :]
    ang = 2.0 * np.pi * ((l * k) % L) / L
    c, s = np.cos(ang), np.sin(ang)
    w_f = np.block([[c, -s], [s, c]])
    w_i = np.block([[c, s], [-s, c]])
    half = L // 2
    s_f = np.zeros((2 * L, 2 * L))
    s_i = np.zeros((2 * L, 2 * L))
    lo = np.arange(half)[None, :]
    hi = np.arange(half, L)[None, :]
    a0 = 2.0 * np.pi * ((l * lo) % L) / L
    a16 = 2.0 * np.pi * ((l * (16 + 32 * hi)) % N) / N
    s_f[:L, :half] = np.cos(a0)
    s_f[:L, L : L + half] = -np.sin(a0)
    s_f[:L, L] = 1.0 - 2.0 * (np.arange(L) % 2)
    s_f[L:, half:L] = np.cos(a16)
    s_f[L:, L + half :] = -np.sin(a16)
    s_i[:half, :L] = 2.0 * np.cos(a0).T
    s_i[L : L + half, :L] = -2.0 * np.sin(a0).T
    s_i[0, :L] = 1.0
    s_i[L, :L] = 1.0 - 2.0 * (np.arange(L) % 2)
    s_i[half:L, L:] = 2.0 * np.cos(a16).T
    s_i[L + half :, L:] = -2.0 * np.sin(a16).T
    mats = np.stack([_split_table(m) for m in (w_f, w_i, s_f.T, s_i)])
    q = np.arange(T)[:, None]
    tw = 2.0 * np.pi * ((q * np.arange(L)[None, :]) % N) / N
    return mats, np.stack([np.cos(tw), -np.sin(tw)]).astype(np.float32)


def times_w(re, im, k, n, sign):
    k %= n
    if k == 0:
        return re, im
    if 4 * k == n:
        return (-im, re) if sign > 0 else (im, -re)
    if 2 * k == n:
        return -re, -im
    r = math.sqrt(0.5)
    if 8 * k == n:
        return ((re - im) * r, (re + im) * r) if sign > 0 else ((re + im) * r, (im - re) * r)
    if 8 * k == 3 * n:
        return ((re + im) * -r, (re - im) * r) if sign > 0 else ((im - re) * r, (re + im) * -r)
    c = math.cos(2.0 * math.pi * k / n)
    s = sign * math.sin(2.0 * math.pi * k / n)
    return re * c - im * s, re * s + im * c


def cfft(vals, sign):
    n = len(vals)
    if n == 1:
        return vals
    even, odd = cfft(vals[0::2], sign), cfft(vals[1::2], sign)
    out = [None] * n
    for k in range(n // 2):
        a, b = even[k]
        c, d = times_w(*odd[k], k, n, sign)
        out[k] = (a + c, b + d)
        out[k + n // 2] = (a - c, b - d)
    return out


def rfft(vals):
    n = len(vals)
    if n == 2:
        return [(vals[0] + vals[1], None), (vals[0] - vals[1], None)]
    even, odd = rfft(vals[0::2]), rfft(vals[1::2])
    out = [None] * (n // 2 + 1)
    for k in range(n // 4 + 1):
        a, b = even[k]
        if k == 0:
            out[0] = (a + odd[0][0], None)
            out[n // 2] = (a - odd[0][0], None)
        elif k == n // 4:
            out[k] = (a, -odd[k][0])
        else:
            c, d = times_w(*odd[k], k, n, -1)
            out[k] = (a + c, b + d)
            out[n // 2 - k] = (a - c, d - b)
    return out


def irfft(bins):
    n = 2 * (len(bins) - 1)
    if n == 2:
        return [bins[0][0] + bins[1][0], bins[0][0] - bins[1][0]]
    even, odd = [None] * (n // 4 + 1), [None] * (n // 4 + 1)
    for k in range(n // 4 + 1):
        a, b = bins[k]
        if k == 0:
            c = bins[n // 2][0]
            even[0], odd[0] = (a + c, None), (a - c, None)
        elif k == n // 4:
            even[k], odd[k] = (2.0 * a, None), (-2.0 * b, None)
        else:
            c, d = bins[n // 2 - k]
            even[k] = (a + c, b - d)
            odd[k] = times_w(a - c, b + d, k, n, 1)
    out = [None] * n
    out[0::2], out[1::2] = irfft(even), irfft(odd)
    return out


def split(v):
    hi = v.astype(BF16)
    return hi, (v - hi.astype(F32)).astype(BF16)


def dot(a, b, nt=False):
    dims = (((1,), (1 if nt else 0,)), ((), ()))
    return lax.dot_general(a, b, dims, preferred_element_type=F32)


def dot3(data, mats, which):
    hi, lo = split(data)
    w_hi, w_lo = mats[which, 0], mats[which, 1]
    return dot(hi, w_hi) + (dot(lo, w_hi) + dot(hi, w_lo))


def field_kernel(
    off, x_hbm, amp_hbm, mats, tw,
    p_hbm, halo_out, up_out,
    x_v, amp_v, a_v, send1, recv1, send2, recv2, z_v, z2_v, amp_t, tmp_t, nyq, nyq_in, pr_v, p_v,
    halo_s, halo_r, bs_main, bs_lead, in_main, in_lead, gsel,
    x_sem, amp_sem, s_sem, r_sem, p_sem, m_sem,
):
    gx, me = lax.axis_index("gx"), lax.axis_index("gy")
    south, north = lax.rem(me + 1, G), lax.rem(me + G - 1, G)

    x_parts = [
        pltpu.make_async_copy(x_hbm.at[pl.ds(64 * i, 64)], x_v.at[pl.ds(64 * i, 64)], x_sem.at[i])
        for i in range(4)
    ]
    for cp in x_parts:
        cp.start()
    amp_parts = [
        pltpu.make_async_copy(amp_hbm.at[:, pl.ds(L * h, L)], amp_v.at[h], amp_sem.at[h]) for h in range(2)
    ]
    for cp in amp_parts:
        cp.start()

    barrier = pltpu.get_barrier_semaphore()
    for o in range(1, G):
        pl.semaphore_signal(barrier, inc=1, device_id={"gy": lax.rem(me + o, G)}, device_id_type=MESH)
    for o in range(1, GX):
        peer = lax.rem(gx + o, GX)
        pl.semaphore_signal(barrier, inc=1, device_id={"gx": peer}, device_id_type=MESH)
        pl.semaphore_signal(barrier, inc=1, device_id={"gx": peer, "gy": south}, device_id_type=MESH)

    def x_tiles(i, carry):
        rows = pl.ds(pl.multiple_of(8 * i, 8), 8)
        bins = rfft([x_v[rows, L * t : L * (t + 1)] for t in range(T)])
        a_v[0, rows, :L] = bins[0][0]
        a_v[0, rows, L:] = bins[T // 2][0]
        for k in range(1, SLOTS):
            a, b = bins[k]
            c, s = tw[0, k : k + 1, :], tw[1, k : k + 1, :]
            a_v[k, rows, :L] = a * c - b * s
            a_v[k, rows, L:] = a * s + b * c
        return carry

    for i in range(4):
        x_parts[i].wait()
        lax.fori_loop(8 * i, 8 * i + 8, x_tiles, 0)

    def peer_copy(src, dst, phase, chunk, o):
        return pltpu.make_async_remote_copy(
            src_ref=src,
            dst_ref=dst,
            send_sem=s_sem.at[phase, chunk, o],
            recv_sem=r_sem.at[phase, chunk, o],
            device_id={"gy": lax.rem(me + o, G)},
            device_id_type=MESH,
        )

    def first_copy(chunk, o):
        d = lax.rem(me + o, G)
        return peer_copy(send1.at[d, pl.ds(PER * chunk, PER)], recv1.at[chunk, me], 0, chunk, o)

    def second_copy(chunk, o):
        d = lax.rem(me + o, G)
        return peer_copy(send2.at[d, pl.ds(PER * chunk, PER)], recv2.at[chunk, me], 1, chunk, o)

    def own_copy(first, chunk):
        src, dst = (send1, recv1) if first else (send2, recv2)
        phase = 0 if first else 1
        return pltpu.make_async_copy(
            src.at[me, pl.ds(PER * chunk, PER)], dst.at[chunk, me], r_sem.at[phase, chunk, 0]
        )

    def x_lanes(slot, carry):
        which = jnp.where(slot == 0, 2, 1)
        hi, lo = split(a_v[slot])
        w_hi, w_lo = mats[which, 0], mats[which, 1]
        o = dot(w_hi, hi, True) + (dot(w_hi, lo, True) + dot(w_lo, hi, True))
        for c in range(2):
            for d in range(G):
                send1[d, slot, c] = o[(c * G + d) * 8 : (c * G + d) * 8 + 8, :]
        return carry

    for chunk in range(CHUNKS):
        lax.fori_loop(PER * chunk, PER * chunk + PER, x_lanes, 0)
        if chunk == 0:
            pl.semaphore_wait(barrier, G - 1 + 2 * (GX - 1))
        for o in range(1, G):
            first_copy(chunk, o).start()
        own_copy(True, chunk).start()

    for cp in amp_parts:
        cp.wait()

    def amp_rows(q, carry):
        for h in range(2):
            block = amp_v[h, pl.ds(q, L, stride=T), :]
            tmp_t[L * h : L * (h + 1), :] = block.T
        first = jnp.where(me < G // 2, tmp_t[pl.ds(0, 8, stride=T), :], tmp_t[pl.ds(16, 8, stride=T), :])
        amp_t[q, 0:8, :] = first * (1.0 / (N * N))
        for k in range(1, SLOTS):
            amp_t[q, 8 * k : 8 * k + 8, :] = tmp_t[pl.ds(k, 8, stride=T), :] * (1.0 / (N * N))
        nyq[q] = tmp_t[0:8, :] * (1.0 / (N * N))
        return carry

    lax.fori_loop(0, T, amp_rows, 0)
    nyq_cp = pltpu.make_async_remote_copy(
        src_ref=nyq, dst_ref=nyq_in, send_sem=m_sem.at[0], recv_sem=m_sem.at[1],
        device_id={"gy": lax.rem(me + G // 2, G)}, device_id_type=MESH,
    )
    nyq_cp.start()
    nyq_cp.wait()

    for chunk in range(CHUNKS):
        for o in range(1, G):
            first_copy(chunk, o).wait_recv()
        own_copy(True, chunk).wait()

        def y_tiles(j, carry, chunk=chunk):
            rows = pl.ds(pl.multiple_of(8 * j, 8), 8)
            vals = [
                tuple(recv1[chunk, t // 2, j, c, :, L * (t % 2) : L * (t % 2 + 1)] for c in range(2))
                for t in range(T)
            ]
            out = cfft(vals, -1)
            for q in range(T):
                a, b = out[q]
                if q > 0:
                    c, s = tw[0, q : q + 1, :], tw[1, q : q + 1, :]
                    a, b = a * c - b * s, a * s + b * c
                z_v[q, rows, :L] = a
                z_v[q, rows, L:] = b
            return carry

        lax.fori_loop(0, PER, y_tiles, 0)

        def y_lanes(b, carry, chunk=chunk):
            qs = pl.ds(8 * b, 8)
            f = dot3(z_v[qs].reshape(8 * 8 * PER, 2 * L), mats, 0)
            amp = amp_t[qs, 8 * PER * chunk : 8 * PER * (chunk + 1), :].reshape(8 * 8 * PER, L)
            filtered = jnp.concatenate([f[:, :L] * amp, f[:, L:] * amp], axis=1)
            z_v[qs] = dot3(filtered, mats, 1).reshape(8, 8 * PER, 2 * L)
            if chunk == 0:

                @pl.when(me == 0)
                def _():
                    other = nyq_in[qs].reshape(64, L)
                    g = f.reshape(8, 8 * PER, 2 * L)[:, :8, :].reshape(64, 2 * L)
                    other = jnp.concatenate([g[:, :L] * other, g[:, L:] * other], axis=1)
                    z2_v[qs] = dot3(other, mats, 1).reshape(8, 8, 2 * L)

            return carry

        lax.fori_loop(0, T // 8, y_lanes, 0)

        def back(get):
            vals = []
            for q in range(T):
                a, b = get(q)
                if q > 0:
                    c, s = tw[0, q : q + 1, :], tw[1, q : q + 1, :]
                    a, b = a * c + b * s, b * c - a * s
                vals.append((a, b))
            return cfft(vals, 1)

        def y_back(j, carry, chunk=chunk):
            rows = pl.ds(pl.multiple_of(8 * j, 8), 8)
            out = back(lambda q: (z_v[q, rows, :L], z_v[q, rows, L:]))
            for t in range(T):
                for c in range(2):
                    send2[t // 2, PER * chunk + j, c, :, L * (t % 2) : L * (t % 2 + 1)] = out[t][c]
            return carry

        lax.fori_loop(0, PER, y_back, 0)
        if chunk == 0:

            @pl.when(me == 0)
            def _():
                out = back(lambda q: (z2_v[q, :, :L], z2_v[q, :, L:]))
                for t in range(T):
                    send2[t // 2, 0, 1, 0:1, L * (t % 2) : L * (t % 2 + 1)] = out[t][1][0:1, :]

        for o in range(1, G):
            second_copy(chunk, o).start()
        own_copy(False, chunk).start()

    for chunk in range(CHUNKS):
        for o in range(1, G):
            second_copy(chunk, o).wait_recv()
        own_copy(False, chunk).wait()

        def x_back(j, carry, chunk=chunk):
            slot = PER * chunk + j
            data = jnp.concatenate(
                [recv2[chunk, d, j, c] for c in range(2) for d in range(G)], axis=0
            )
            which = jnp.where(slot == 0, 3, 1)
            o = dot3(data.T, mats, which)
            a, b = o[:, :L], o[:, L:]
            c, s = tw[0, pl.ds(slot, 1), :], tw[1, pl.ds(slot, 1), :]
            a_v[slot, :, :L] = a * c + b * s
            a_v[slot, :, L:] = b * c - a * s
            return carry

        lax.fori_loop(0, PER, x_back, 0)

    pr_v[:, :, ROWS : ROWS + 8, :] = jnp.zeros((2, T, 8, L), F32)

    def x_last(i, carry):
        rows = pl.ds(pl.multiple_of(8 * i, 8), 8)
        bins = [(a_v[0, rows, :L], None)]
        bins += [(a_v[k, rows, :L], a_v[k, rows, L:]) for k in range(1, SLOTS)]
        bins += [(a_v[0, rows, L:], None)]
        out = irfft(bins)
        for t in range(T):
            p = jnp.exp(out[t])
            p_v[rows, L * t : L * (t + 1)] = p
            pr_v[0, t, rows, :] = p
            pr_v[1, t, rows, :] = 1.0 / p
        return carry

    x_last(0, 0)
    for t in range(T):
        halo_s[t : t + 1, :] = p_v[0:1, L * t : L * (t + 1)]
    halo_cp = pltpu.make_async_remote_copy(
        src_ref=halo_s, dst_ref=halo_r, send_sem=m_sem.at[2], recv_sem=m_sem.at[3],
        device_id={"gy": north}, device_id_type=MESH,
    )
    halo_cp.start()
    p_parts = []
    for i in range(4):
        lax.fori_loop(max(8 * i, 1), 8 * i + 8, x_last, 0)
        cp = pltpu.make_async_copy(p_v.at[pl.ds(64 * i, 64)], p_hbm.at[pl.ds(64 * i, 64)], p_sem.at[i])
        cp.start()
        p_parts.append(cp)

    shift_y, shift_x = off[0], off[1]
    wide = 1024 + L
    gsel[...] = jnp.where(
        (lax.broadcasted_iota(jnp.int32, (wide, L), 0) - shift_x) // 8
        == lax.broadcasted_iota(jnp.int32, (wide, L), 1),
        1.0,
        0.0,
    ).astype(BF16)
    lead_mask = lax.broadcasted_iota(jnp.int32, (8, L), 0) < shift_y
    for v in range(2):

        def y_sums(t, carry, v=v):
            lanes = pl.ds(pl.multiple_of(L * t, L), L)
            total = jnp.zeros((T, L), F32)
            for a in range(8):
                here = pr_v[v, t, pl.ds(a, T, stride=8), :]
                after = pr_v[v, t, pl.ds(a + 8, T, stride=8), :]
                total += jnp.where(a >= shift_y, here, after)
            x_v[40 * v : 40 * v + T, lanes] = total
            x_v[40 * v + T : 40 * v + 40, lanes] = jnp.where(lead_mask, pr_v[v, t, 0:8, :], 0.0)
            return carry

        lax.fori_loop(0, T, y_sums, 0)

    g = gsel[...]
    for b in range(4):
        lanes = [x_v[0:80, 1024 * b : 1024 * (b + 1)]]
        nxt = 1024 * (b + 1) % N
        lanes.append(x_v[0:80, nxt : nxt + L])
        hi, lo = split(jnp.concatenate(lanes, axis=1))
        out = dot(hi, g) + dot(lo, g)
        for v in range(2):
            bs_main[b, v] = out[40 * v : 40 * v + T, :]
            bs_lead[b, v] = out[40 * v + T : 40 * v + 40, :]

    def main_copy(o):
        peer = lax.rem(gx + o, GX)
        return pltpu.make_async_remote_copy(
            src_ref=bs_main.at[peer // 2], dst_ref=in_main.at[gx],
            send_sem=m_sem.at[8 + o], recv_sem=m_sem.at[16 + o],
            device_id={"gx": peer}, device_id_type=MESH,
        )

    def lead_copy(o):
        peer = lax.rem(gx + o, GX)
        return pltpu.make_async_remote_copy(
            src_ref=bs_lead.at[peer // 2], dst_ref=in_lead.at[gx],
            send_sem=m_sem.at[24 + o], recv_sem=m_sem.at[32 + o],
            device_id={"gx": peer, "gy": north}, device_id_type=MESH,
        )

    own_main = pltpu.make_async_copy(bs_main.at[gx // 2], in_main.at[gx], m_sem.at[16])
    own_main.start()
    for o in range(1, GX):
        main_copy(o).start()
    for o in range(GX):
        lead_copy(o).start()

    halo_cp.wait()
    for t in range(T):
        halo_out[0:1, L * t : L * (t + 1)] = halo_r[t : t + 1, :]

    own_main.wait()
    for o in range(1, GX):
        main_copy(o).wait()
    for o in range(GX):
        lead_copy(o).wait()
    sums = []
    last = lax.broadcasted_iota(jnp.int32, (T, L), 0) == T - 1
    for v in range(2):
        main, lead = in_main[0, v], in_lead[0, v]
        for g_ in range(1, GX):
            main += in_main[g_, v]
            lead += in_lead[g_, v]
        lead = jnp.sum(lead, axis=0, keepdims=True)
        sums.append(main + jnp.where(last, jnp.broadcast_to(lead, (T, L)), 0.0))
    up = jnp.sqrt(sums[0] / sums[1])
    up_out[...] = jnp.where(lax.rem(gx, 2) == 0, up[:, : L // 2], up[:, L // 2 :])

    for cp in p_parts:
        cp.wait()
    for chunk in range(CHUNKS):
        for o in range(1, G):
            first_copy(chunk, o).wait_send()
            second_copy(chunk, o).wait_send()


def field(off, x, amp, mats, tw):
    any_spec = pl.BlockSpec(memory_space=pl.ANY)
    vmem = pl.BlockSpec(memory_space=pltpu.VMEM)
    piece = (2, 8, ROWS)
    return pl.pallas_call(
        field_kernel,
        out_shape=(
            jax.ShapeDtypeStruct((ROWS, N), F32),
            jax.ShapeDtypeStruct((1, N), F32),
            jax.ShapeDtypeStruct((T, L // 2), F32),
        ),
        in_specs=[pl.BlockSpec(memory_space=pltpu.SMEM), any_spec, any_spec, vmem, vmem],
        out_specs=(any_spec, vmem, vmem),
        scratch_shapes=[
            pltpu.VMEM((ROWS, N), F32),
            pltpu.VMEM((2, N, L), F32),
            pltpu.VMEM((SLOTS, ROWS, 2 * L), F32),
            pltpu.VMEM((G, SLOTS) + piece, F32),
            pltpu.VMEM((CHUNKS, G, PER) + piece, F32),
            pltpu.VMEM((G, SLOTS) + piece, F32),
            pltpu.VMEM((CHUNKS, G, PER) + piece, F32),
            pltpu.VMEM((T, 8 * PER, 2 * L), F32),
            pltpu.VMEM((T, 8, 2 * L), F32),
            pltpu.VMEM((T, 8 * SLOTS, L), F32),
            pltpu.VMEM((2 * L, L), F32),
            pltpu.VMEM((T, 8, L), F32),
            pltpu.VMEM((T, 8, L), F32),
            pltpu.VMEM((2, T, ROWS + 8, L), F32),
            pltpu.VMEM((ROWS, N), F32),
            pltpu.VMEM((T, L), F32),
            pltpu.VMEM((T, L), F32),
            pltpu.VMEM((4, 2, T, L), F32),
            pltpu.VMEM((4, 2, 8, L), F32),
            pltpu.VMEM((GX, 2, T, L), F32),
            pltpu.VMEM((GX, 2, 8, L), F32),
            pltpu.VMEM((1024 + L, L), BF16),
            pltpu.SemaphoreType.DMA((4,)),
            pltpu.SemaphoreType.DMA((2,)),
            pltpu.SemaphoreType.DMA((2, CHUNKS, G)),
            pltpu.SemaphoreType.DMA((2, CHUNKS, G)),
            pltpu.SemaphoreType.DMA((4,)),
            pltpu.SemaphoreType.DMA((40,)),
        ],
        compiler_params=pltpu.CompilerParams(
            collective_id=0, has_side_effects=True, vmem_limit_bytes=60 << 20
        ),
        name="field",
    )(off, x, amp, mats, tw)


BLOCK = 32


def trans_kernel(p_ref, next_ref, halo_ref, tx_ref, ty_ref):
    p = p_ref[...]
    q = pltpu.roll(p, N - 1, 1)
    tx_ref[...] = 2.0 * p * q / (p + q)
    edge = pl.program_id(0) == pl.num_programs(0) - 1
    row = jnp.where(edge, halo_ref[...], next_ref[0:1, :])
    q = jnp.concatenate([p[1:, :], row], axis=0)
    ty_ref[...] = 2.0 * p * q / (p + q)


def transmissibilities(p, halo):
    steps = ROWS // BLOCK
    block = pl.BlockSpec((BLOCK, N), lambda i: (i, 0))
    after = pl.BlockSpec((8, N), lambda i: (jnp.minimum((i + 1) * (BLOCK // 8), ROWS // 8 - 1), 0))
    return pl.pallas_call(
        trans_kernel,
        grid=(steps,),
        out_shape=(jax.ShapeDtypeStruct((ROWS, N), F32),) * 2,
        in_specs=[block, after, pl.BlockSpec((1, N), lambda i: (0, 0))],
        out_specs=(block, block),
        compiler_params=pltpu.CompilerParams(vmem_limit_bytes=32 << 20),
        name="trans",
    )(p, p, halo)


def shards(white_noise, amplitude, offsets):
    mats, tw = tables()
    p, halo, upscaled = field(offsets, white_noise[0], amplitude, jnp.asarray(mats), jnp.asarray(tw))
    trans_x, trans_y = transmissibilities(p, halo)
    return trans_x[None], trans_y[None], upscaled


def solution(mesh):
    return jax.shard_map(
        shards,
        mesh=mesh,
        in_specs=(P("gx", "gy", None), P(None, "gy"), P()),
        out_specs=(P("gx", "gy", None), P("gx", "gy", None), P("gy", "gx")),
        check_vma=False,
    )
```

```python
import functools
import math

import jax
import jax.numpy as jnp
import numpy as np
from jax import lax
from jax.experimental import pallas as pl
from jax.experimental.pallas import tpu as pltpu
from jax.sharding import PartitionSpec as P

MESH = pl.DeviceIdType.MESH
F32 = jnp.float32
BF16 = jnp.bfloat16
L = 128
T = 32
N = L * T
SLOTS = 16
PER = 4
CHUNKS = SLOTS // PER
G = 16
GX = 8
ROWS = N // G
ORDER = [2, 4, 12, 14, 8, 6, 10, 3, 13, 5, 11, 9, 7, 15, 1]


def _split_table(m):
    hi = m.astype(jnp.bfloat16)
    lo = (m - hi.astype(np.float64)).astype(jnp.bfloat16)
    return np.stack([np.asarray(hi), np.asarray(lo)])


def tables():
    l = np.arange(L)[:, None]
    k = np.arange(L)[None, :]
    ang = 2.0 * np.pi * ((l * k) % L) / L
    c, s = np.cos(ang), np.sin(ang)
    w_f = np.block([[c, -s], [s, c]])
    w_i = np.block([[c, s], [-s, c]])
    half = L // 2
    s_f = np.zeros((2 * L, 2 * L))
    s_i = np.zeros((2 * L, 2 * L))
    lo = np.arange(half)[None, :]
    hi = np.arange(half, L)[None, :]
    a0 = 2.0 * np.pi * ((l * lo) % L) / L
    a16 = 2.0 * np.pi * ((l * (16 + 32 * hi)) % N) / N
    s_f[:L, :half] = np.cos(a0)
    s_f[:L, L : L + half] = -np.sin(a0)
    s_f[:L, L] = 1.0 - 2.0 * (np.arange(L) % 2)
    s_f[L:, half:L] = np.cos(a16)
    s_f[L:, L + half :] = -np.sin(a16)
    s_i[:half, :L] = 2.0 * np.cos(a0).T
    s_i[L : L + half, :L] = -2.0 * np.sin(a0).T
    s_i[0, :L] = 1.0
    s_i[L, :L] = 1.0 - 2.0 * (np.arange(L) % 2)
    s_i[half:L, L:] = 2.0 * np.cos(a16).T
    s_i[L + half :, L:] = -2.0 * np.sin(a16).T
    mats = np.stack([_split_table(m) for m in (w_f, w_i, s_f.T, s_i)])
    q = np.arange(T)[:, None]
    tw = 2.0 * np.pi * ((q * np.arange(L)[None, :]) % N) / N
    return mats, np.stack([np.cos(tw), -np.sin(tw)]).astype(np.float32)


def slot_of(chunk, j):
    return PER * ((chunk + 1) % CHUNKS) + j


def times_w(re, im, k, n, sign):
    k %= n
    if k == 0:
        return re, im
    if 4 * k == n:
        return (-im, re) if sign > 0 else (im, -re)
    if 2 * k == n:
        return -re, -im
    r = math.sqrt(0.5)
    if 8 * k == n:
        return ((re - im) * r, (re + im) * r) if sign > 0 else ((re + im) * r, (im - re) * r)
    if 8 * k == 3 * n:
        return ((re + im) * -r, (re - im) * r) if sign > 0 else ((im - re) * r, (re + im) * -r)
    c = math.cos(2.0 * math.pi * k / n)
    s = sign * math.sin(2.0 * math.pi * k / n)
    return re * c - im * s, re * s + im * c


def cfft(vals, sign):
    n = len(vals)
    if n == 1:
        return vals
    even, odd = cfft(vals[0::2], sign), cfft(vals[1::2], sign)
    out = [None] * n
    for k in range(n // 2):
        a, b = even[k]
        c, d = times_w(*odd[k], k, n, sign)
        out[k] = (a + c, b + d)
        out[k + n // 2] = (a - c, b - d)
    return out


def rfft(vals):
    n = len(vals)
    if n == 2:
        return [(vals[0] + vals[1], None), (vals[0] - vals[1], None)]
    even, odd = rfft(vals[0::2]), rfft(vals[1::2])
    out = [None] * (n // 2 + 1)
    for k in range(n // 4 + 1):
        a, b = even[k]
        if k == 0:
            out[0] = (a + odd[0][0], None)
            out[n // 2] = (a - odd[0][0], None)
        elif k == n // 4:
            out[k] = (a, -odd[k][0])
        else:
            c, d = times_w(*odd[k], k, n, -1)
            out[k] = (a + c, b + d)
            out[n // 2 - k] = (a - c, d - b)
    return out


def irfft(bins):
    n = 2 * (len(bins) - 1)
    if n == 2:
        return [bins[0][0] + bins[1][0], bins[0][0] - bins[1][0]]
    even, odd = [None] * (n // 4 + 1), [None] * (n // 4 + 1)
    for k in range(n // 4 + 1):
        a, b = bins[k]
        if k == 0:
            c = bins[n // 2][0]
            even[0], odd[0] = (a + c, None), (a - c, None)
        elif k == n // 4:
            even[k], odd[k] = (2.0 * a, None), (-2.0 * b, None)
        else:
            c, d = bins[n // 2 - k]
            even[k] = (a + c, b - d)
            odd[k] = times_w(a - c, b + d, k, n, 1)
    out = [None] * n
    out[0::2], out[1::2] = irfft(even), irfft(odd)
    return out


def split(v):
    hi = v.astype(BF16)
    return hi, (v - hi.astype(F32)).astype(BF16)


def dot(a, b, nt=False):
    dims = (((1,), (1 if nt else 0,)), ((), ()))
    return lax.dot_general(a, b, dims, preferred_element_type=F32)


def dot3(data, mats, which):
    hi, lo = split(data)
    w_hi, w_lo = mats[which, 0], mats[which, 1]
    return dot(hi, w_hi) + (dot(lo, w_hi) + dot(hi, w_lo))


def field_kernel(
    off_hbm, x_hbm, amp_hbm, mats_hbm, tw_hbm,
    tx_out, ty_out, ratio_out,
    off, tw, mats, p_v, a_v, send1, recv1, send2, recv2, z_v, z2_v, amp_t, tmp_t, nyq, nyq_in, pr_v,
    up_s, low_s, sum_s, halo_s, halo_r, bs_main, in_main, gsel,
    x_sem, amp_sem, s1_sem, r1_sem, s2_sem, r2_sem, m_sem,
):
    gx, me = lax.axis_index("gx"), lax.axis_index("gy")
    north = lax.rem(me + G - 1, G)

    barrier = pltpu.get_barrier_semaphore()
    for o in ORDER:
        pl.semaphore_signal(barrier, inc=1, device_id={"gy": lax.rem(me + o, G)}, device_id_type=MESH)
    for o in range(1, GX):
        pl.semaphore_signal(barrier, inc=1, device_id={"gx": lax.rem(gx + o, GX)}, device_id_type=MESH)

    x_parts = [
        pltpu.make_async_copy(x_hbm.at[pl.ds(32 * i, 32)], p_v.at[pl.ds(32 * i, 32)], x_sem.at[i])
        for i in range(8)
    ]
    mats_cp = pltpu.make_async_copy(mats_hbm, mats, amp_sem.at[2])
    tw_cp = pltpu.make_async_copy(tw_hbm, tw, amp_sem.at[3])
    off_cp = pltpu.make_async_copy(off_hbm, off, amp_sem.at[4])
    x_parts[0].start()
    tw_cp.start()
    x_parts[1].start()
    mats_cp.start()
    off_cp.start()
    for cp in x_parts[2:]:
        cp.start()
    amp_parts = [
        pltpu.make_async_copy(amp_hbm.at[:, pl.ds(L * h, L)], pr_v.at[0, pl.ds(N * h, N)], amp_sem.at[h]) for h in range(2)
    ]
    for cp in amp_parts:
        cp.start()

    def x_tiles(i, carry):
        rows = pl.ds(pl.multiple_of(8 * i, 8), 8)
        bins = rfft([p_v[rows, L * t : L * (t + 1)] for t in range(T)])
        a_v[0, rows, :L] = bins[0][0]
        a_v[0, rows, L:] = bins[T // 2][0]
        for k in range(1, SLOTS):
            a, b = bins[k]
            c, s = tw[0, k : k + 1, :], tw[1, k : k + 1, :]
            a_v[k, rows, :L] = a * c - b * s
            a_v[k, rows, L:] = a * s + b * c
        return carry

    def first_copy(chunk, o):
        d = lax.rem(me + o, G)
        return pltpu.make_async_remote_copy(
            src_ref=send1.at[d, chunk], dst_ref=recv1.at[chunk, me],
            send_sem=s1_sem.at[chunk, o], recv_sem=r1_sem.at[chunk, o],
            device_id={"gy": d}, device_id_type=MESH,
        )

    def first_own(chunk):
        return pltpu.make_async_copy(send1.at[me, chunk], recv1.at[chunk, me], r1_sem.at[chunk, 0])

    def send_first(chunk):
        for o in ORDER:
            first_copy(chunk, o).start()
        first_own(chunk).start()

    def second_copy(half, chunk, o):
        d = lax.rem(me + o, G)
        return pltpu.make_async_remote_copy(
            src_ref=send2.at[d, half, chunk], dst_ref=recv2.at[half, chunk, me],
            send_sem=s2_sem.at[half, chunk, o], recv_sem=r2_sem.at[half, chunk, o],
            device_id={"gy": d}, device_id_type=MESH,
        )

    def second_own(half, chunk):
        return pltpu.make_async_copy(
            send2.at[me, half, chunk], recv2.at[half, chunk, me], r2_sem.at[half, chunk, 0]
        )

    def send_second(half, chunk):
        for o in ORDER:
            second_copy(half, chunk, o).start()
        second_own(half, chunk).start()

    def x_lanes(j, carry, chunk):
        slot = slot_of(chunk, j)
        which = jnp.where(slot == 0, 2, 1)
        hi, lo = split(a_v[slot])
        w_hi, w_lo = mats[which, 0], mats[which, 1]
        o = dot(w_hi, hi, True) + (dot(w_hi, lo, True) + dot(w_lo, hi, True))
        for h in range(2):
            for c in range(2):
                for d in range(G):
                    r = (c * G + d) * 8
                    send1[d, chunk, h, j, c] = o[r : r + 8, L * h : L * (h + 1)]
        return carry

    for i in range(8):
        x_parts[i].wait()
        if i == 0:
            tw_cp.wait()
        lax.fori_loop(4 * i, 4 * i + 4, x_tiles, 0)
    mats_cp.wait()
    off_cp.wait()
    for chunk in range(CHUNKS):
        lax.fori_loop(0, PER, functools.partial(x_lanes, chunk=chunk), 0)
        if chunk == 0:
            pl.semaphore_wait(barrier, G - 1 + GX - 1)
        send_first(chunk)

    for cp in amp_parts:
        cp.wait()

    def amp_rows(q, carry):
        for h in range(2):
            block = pr_v[0, pl.ds(N * h + q, L, stride=T), :]
            tmp_t[L * h : L * (h + 1), :] = block.T
        first = jnp.where(me < G // 2, tmp_t[pl.ds(0, 8, stride=T), :], tmp_t[pl.ds(16, 8, stride=T), :])
        amp_t[q, 0:8, :] = first * (1.0 / (N * N))
        for k in range(1, SLOTS):
            amp_t[q, 8 * k : 8 * k + 8, :] = tmp_t[pl.ds(k, 8, stride=T), :] * (1.0 / (N * N))
        nyq[pl.ds(q, 1), :] = tmp_t[0:1, :] * (1.0 / (N * N))
        return carry

    lax.fori_loop(0, T, amp_rows, 0)
    nyq_cp = pltpu.make_async_remote_copy(
        src_ref=nyq, dst_ref=nyq_in, send_sem=m_sem.at[0], recv_sem=m_sem.at[1],
        device_id={"gy": 0}, device_id_type=MESH,
    )

    @pl.when(me == G // 2)
    def _():
        nyq_cp.start()
        nyq_cp.wait_send()


    shift_y, shift_x = off[0], off[1]
    wide = 1024 + L
    gsel[...] = jnp.where(
        (lax.broadcasted_iota(jnp.int32, (wide, L), 0) - shift_x) // 8
        == lax.broadcasted_iota(jnp.int32, (wide, L), 1),
        1.0,
        0.0,
    ).astype(BF16)

    for chunk in range(CHUNKS):
        for o in ORDER:
            first_copy(chunk, o).wait_recv()
        first_own(chunk).wait()

        def y_tiles(j, carry, chunk=chunk):
            rows = pl.ds(pl.multiple_of(8 * j, 8), 8)
            vals = [tuple(recv1[chunk, t // 2, t % 2, j, c] for c in range(2)) for t in range(T)]
            out = cfft(vals, -1)
            for q in range(T):
                a, b = out[q]
                if q > 0:
                    c, s = tw[0, q : q + 1, :], tw[1, q : q + 1, :]
                    a, b = a * c - b * s, a * s + b * c
                z_v[q, rows, :L] = a
                z_v[q, rows, L:] = b
            return carry

        lax.fori_loop(0, PER, y_tiles, 0)
        if chunk == CHUNKS - 1:

            @pl.when(me == 0)
            def _():
                nyq_cp.wait_recv()

        def y_lanes(b, carry, chunk=chunk):
            qs = pl.ds(8 * b, 8)
            f = dot3(z_v[qs].reshape(8 * 8 * PER, 2 * L), mats, 0)
            first = 8 * slot_of(chunk, 0)
            amp = amp_t[qs, first : first + 8 * PER, :].reshape(8 * 8 * PER, L)
            filtered = jnp.concatenate([f[:, :L] * amp, f[:, L:] * amp], axis=1)
            z_v[qs] = dot3(filtered, mats, 1).reshape(8, 8 * PER, 2 * L)
            if chunk == CHUNKS - 1:

                @pl.when(me == 0)
                def _():
                    other = nyq_in[qs]
                    other = jnp.broadcast_to(other[:, None, :], (8, 8, L)).reshape(64, L)
                    g = f.reshape(8, 8 * PER, 2 * L)[:, :8, :].reshape(64, 2 * L)
                    other = jnp.concatenate([g[:, :L] * other, g[:, L:] * other], axis=1)
                    z2_v[qs] = dot3(other, mats, 1).reshape(8, 8, 2 * L)

            return carry

        lax.fori_loop(0, T // 8, y_lanes, 0)

        def back(get):
            vals = []
            for q in range(T):
                a, b = get(q)
                if q > 0:
                    c, s = tw[0, q : q + 1, :], tw[1, q : q + 1, :]
                    a, b = a * c + b * s, b * c - a * s
                vals.append((a, b))
            return cfft(vals, 1)

        def y_back(j, carry, chunk=chunk):
            rows = pl.ds(pl.multiple_of(8 * j, 8), 8)
            out = back(lambda q: (z_v[q, rows, :L], z_v[q, rows, L:]))
            for t in range(T):
                for c in range(2):
                    send2[t // 2, t % 2, chunk, j, c] = out[t][c]
            return carry

        lax.fori_loop(0, PER, y_back, 0)
        if chunk == CHUNKS - 1:

            @pl.when(me == 0)
            def _():
                out = back(lambda q: (z2_v[q, :, :L], z2_v[q, :, L:]))
                for t in range(T):
                    send2[t // 2, t % 2, CHUNKS - 1, 0, 1, 0:1, :] = out[t][1][0:1, :]

        send_second(0, chunk)
    for chunk in range(CHUNKS):
        send_second(1, chunk)

    def x_back(j, carry, half, chunk):
        slot = slot_of(chunk, j)
        data = jnp.concatenate(
            [recv2[half, chunk, d, j, c] for c in range(2) for d in range(G)], axis=0
        )
        which = jnp.where(slot == 0, 3, 1)
        o = dot3(data.T, mats, which)
        a, b = o[:, :L], o[:, L:]
        c, s = tw[0, pl.ds(slot, 1), :], tw[1, pl.ds(slot, 1), :]
        a_v[slot, L * half : L * (half + 1), :L] = a * c + b * s
        a_v[slot, L * half : L * (half + 1), L:] = b * c - a * s
        return carry

    def x_last(i, carry):
        rows = pl.ds(pl.multiple_of(8 * i, 8), 8)
        bins = [(a_v[0, rows, :L], None)]
        bins += [(a_v[k, rows, :L], a_v[k, rows, L:]) for k in range(1, SLOTS)]
        bins += [(a_v[0, rows, L:], None)]
        out = irfft(bins)
        for t in range(T):
            p = jnp.exp(out[t])
            p_v[rows, L * t : L * (t + 1)] = p
            here = pl.ds(pl.multiple_of(ROWS * t + 8 * i, 8), 8)
            pr_v[0, here, :] = p
            pr_v[1, here, :] = 1.0 / p
        return carry

    def y_sums(t, carry, half):
        for v in range(2):
            up, low = jnp.zeros((16, L), F32), jnp.zeros((16, L), F32)
            for a in range(8):
                u = pr_v[v, pl.ds(ROWS * t + L * half + a, 16, stride=8), :]
                up += jnp.where(a >= shift_y, u, 0.0)
                low += jnp.where(a < shift_y, u, 0.0)
            up_s[v, t, 16 * half : 16 * half + 16, :] = up
            low_s[v, t, 16 * half : 16 * half + 16, :] = low
        return carry

    lane_end = lax.broadcasted_iota(jnp.int32, (8, L), 1) == L - 1

    def trans(i, carry):
        rows = pl.ds(pl.multiple_of(8 * i, 8), 8)
        after = pl.ds(pl.multiple_of(8 * i + 8, 8), 8)
        p = [p_v[rows, L * t : L * (t + 1)] for t in range(T)]
        rolled = [pltpu.roll(v, L - 1, 1) for v in p]
        for t in range(T):
            lanes = slice(L * t, L * (t + 1))
            q = jnp.where(lane_end, rolled[(t + 1) % T], rolled[t])
            tx_out[rows, lanes] = 2.0 * p[t] * q / (p[t] + q)
            q = jnp.concatenate([p[t], p_v[after, lanes]], axis=0)[1:9]
            ty_out[rows, lanes] = 2.0 * p[t] * q / (p[t] + q)
        return carry

    halo_cp = pltpu.make_async_remote_copy(
        src_ref=halo_s, dst_ref=halo_r, send_sem=m_sem.at[2], recv_sem=m_sem.at[3],
        device_id={"gy": north}, device_id_type=MESH,
    )
    g = gsel[...]

    def along_x(rows):
        outs = []
        for b in range(4):
            nxt = 1024 * (b + 1) % N
            lanes = [sum_s[rows, 1024 * b : 1024 * (b + 1)], sum_s[rows, nxt : nxt + L]]
            hi, lo = split(jnp.concatenate(lanes, axis=1))
            outs.append(dot(hi, g) + dot(lo, g))
        return outs

    last_row = lax.broadcasted_iota(jnp.int32, (T, L), 0) == T - 1
    for half in range(2):
        for chunk in range(CHUNKS):
            for o in ORDER:
                second_copy(half, chunk, o).wait_recv()
            second_own(half, chunk).wait()
            lax.fori_loop(0, PER, functools.partial(x_back, half=half, chunk=chunk), 0)
        lax.fori_loop(16 * half, 16 * half + 16, x_last, 0)
        lax.fori_loop(0, T, functools.partial(y_sums, half=half), 0)
        if half == 0:
            for t in range(T):
                halo_s[t : t + 1, :] = p_v[0:1, L * t : L * (t + 1)]
                for v in range(2):
                    sum_s[v : v + 1, L * t : L * (t + 1)] = low_s[v, t, 0:1, :]
            sum_s[2:8, :] = jnp.zeros((6, N), F32)
            for b, out in enumerate(along_x(slice(0, 8))):
                halo_s[T + 2 * b : T + 2 * b + 2, :] = out[0:2]
            halo_cp.start()
            lax.fori_loop(0, 15, trans, 0)

    for t in range(T):
        for v in range(2):
            moved = jnp.where(last_row, 0.0, pltpu.roll(low_s[v, t], T - 1, 0))
            sum_s[T * v : T * v + T, L * t : L * (t + 1)] = up_s[v, t] + moved
    halo_cp.wait()
    for b, out in enumerate(along_x(slice(0, 2 * T))):
        for v in range(2):
            lead = jnp.broadcast_to(halo_r[T + 2 * b + v : T + 2 * b + v + 1, :], (T, L))
            bs_main[b, v] = out[T * v : T * v + T, :] + jnp.where(last_row, lead, 0.0)

    def main_copy(o):
        peer = lax.rem(gx + o, GX)
        return pltpu.make_async_remote_copy(
            src_ref=bs_main.at[peer // 2], dst_ref=in_main.at[gx],
            send_sem=m_sem.at[8 + o], recv_sem=m_sem.at[16 + o],
            device_id={"gx": peer}, device_id_type=MESH,
        )

    own_main = pltpu.make_async_copy(bs_main.at[gx // 2], in_main.at[gx], m_sem.at[16])
    own_main.start()
    for o in range(1, GX):
        main_copy(o).start()
    for t in range(T):
        p_v[ROWS : ROWS + 1, L * t : L * (t + 1)] = halo_r[t : t + 1, :]

    lax.fori_loop(15, 32, trans, 0)
    for chunk in range(CHUNKS):
        for o in ORDER:
            first_copy(chunk, o).wait_send()
    for half in range(2):
        for chunk in range(CHUNKS):
            for o in ORDER:
                second_copy(half, chunk, o).wait_send()

    own_main.wait()
    for o in range(1, GX):
        main_copy(o).wait()
    sums = []
    for v in range(2):
        main = in_main[0, v]
        for g_ in range(1, GX):
            main += in_main[g_, v]
        sums.append(main)
    ratio = sums[0] / sums[1]
    ratio_out[...] = jnp.where(lax.rem(gx, 2) == 0, ratio[:, : L // 2], ratio[:, L // 2 :])


def field(off, x, amp, mats, tw):
    hbm = pl.BlockSpec(memory_space=pltpu.HBM)
    vmem = pl.BlockSpec(memory_space=pltpu.VMEM)
    piece = (PER, 2, 8, L)
    return pl.pallas_call(
        field_kernel,
        out_shape=(
            jax.ShapeDtypeStruct((ROWS, N), F32),
            jax.ShapeDtypeStruct((ROWS, N), F32),
            jax.ShapeDtypeStruct((T, L // 2), F32),
        ),
        in_specs=[hbm] * 5,
        out_specs=(vmem, vmem, vmem),
        scratch_shapes=[
            pltpu.SMEM((2,), jnp.int32),
            pltpu.VMEM(tw.shape, F32),
            pltpu.VMEM(mats.shape, BF16),
            pltpu.VMEM((ROWS + 8, N), F32),
            pltpu.VMEM((SLOTS, ROWS, 2 * L), F32),
            pltpu.VMEM((G, CHUNKS, 2) + piece, F32),
            pltpu.VMEM((CHUNKS, G, 2) + piece, F32),
            pltpu.VMEM((G, 2, CHUNKS) + piece, F32),
            pltpu.VMEM((2, CHUNKS, G) + piece, F32),
            pltpu.VMEM((T, 8 * PER, 2 * L), F32),
            pltpu.VMEM((T, 8, 2 * L), F32),
            pltpu.VMEM((T, 8 * SLOTS, L), F32),
            pltpu.VMEM((2 * L, L), F32),
            pltpu.VMEM((T, L), F32),
            pltpu.VMEM((T, L), F32),
            pltpu.VMEM((2, T * ROWS, L), F32),
            pltpu.VMEM((2, T, T, L), F32),
            pltpu.VMEM((2, T, T, L), F32),
            pltpu.VMEM((2 * T, N), F32),
            pltpu.VMEM((T + 8, L), F32),
            pltpu.VMEM((T + 8, L), F32),
            pltpu.VMEM((4, 2, T, L), F32),
            pltpu.VMEM((GX, 2, T, L), F32),
            pltpu.VMEM((1024 + L, L), BF16),
            pltpu.SemaphoreType.DMA((8,)),
            pltpu.SemaphoreType.DMA((5,)),
            pltpu.SemaphoreType.DMA((CHUNKS, G)),
            pltpu.SemaphoreType.DMA((CHUNKS, G)),
            pltpu.SemaphoreType.DMA((2, CHUNKS, G)),
            pltpu.SemaphoreType.DMA((2, CHUNKS, G)),
            pltpu.SemaphoreType.DMA((24,)),
        ],
        compiler_params=pltpu.CompilerParams(
            collective_id=0, has_side_effects=True, vmem_limit_bytes=44 << 20
        ),
        name="field",
    )(*(pltpu.with_memory_space_constraint(v, pltpu.HBM) for v in (off, x, amp, mats, tw)))


def write_kernel(tx, ty, ratio, tx_out, ty_out, up_out, sem):
    copies = []
    for n, (src, dst) in enumerate(((tx, tx_out), (ty, ty_out))):
        for i in range(4):
            rows = pl.ds(ROWS // 4 * i, ROWS // 4)
            copies.append(pltpu.make_async_copy(src.at[rows], dst.at[rows], sem.at[4 * n + i]))
    for cp in copies:
        cp.start()
    up_out[...] = jnp.sqrt(ratio[...])
    for cp in copies:
        cp.wait()


def written(tx, ty, ratio):
    hbm = pl.BlockSpec(memory_space=pltpu.HBM)
    vmem = pl.BlockSpec(memory_space=pltpu.VMEM)
    return pl.pallas_call(
        write_kernel,
        out_shape=(
            jax.ShapeDtypeStruct((ROWS, N), F32),
            jax.ShapeDtypeStruct((ROWS, N), F32),
            jax.ShapeDtypeStruct((T, L // 2), F32),
        ),
        in_specs=[pl.BlockSpec(memory_space=pl.ANY)] * 2 + [vmem],
        out_specs=(hbm, hbm, vmem),
        scratch_shapes=[pltpu.SemaphoreType.DMA((8,))],
        compiler_params=pltpu.CompilerParams(vmem_limit_bytes=1 << 20),
        name="write",
    )(tx, ty, ratio)


def shards(white_noise, amplitude, offsets):
    mats, tw = tables()
    tx, ty, ratio = field(offsets, white_noise[0], amplitude, jnp.asarray(mats), jnp.asarray(tw))
    trans_x, trans_y, upscaled = written(tx, ty, ratio)
    return trans_x[None], trans_y[None], upscaled


def solution(mesh):
    return jax.shard_map(
        shards,
        mesh=mesh,
        in_specs=(P("gx", "gy", None), P(None, "gy"), P()),
        out_specs=(P("gx", "gy", None), P("gx", "gy", None), P("gy", "gx")),
        check_vma=False,
    )
```

```python
import functools
import math

import jax
import jax.numpy as jnp
import numpy as np
from jax import lax
from jax.experimental import pallas as pl
from jax.experimental.pallas import tpu as pltpu
from jax.sharding import PartitionSpec as P

MESH = pl.DeviceIdType.MESH
F32 = jnp.float32
BF16 = jnp.bfloat16
L = 128
T = 32
N = L * T
SLOTS = 16
PER = 4
CHUNKS = SLOTS // PER
G = 16
GX = 8
ROWS = N // G
ORDER = [2, 4, 12, 14, 8, 6, 10, 3, 13, 5, 11, 9, 7, 15, 1]


def _split_table(m):
    hi = m.astype(jnp.bfloat16)
    lo = (m - hi.astype(np.float64)).astype(jnp.bfloat16)
    return np.stack([np.asarray(hi), np.asarray(lo)])


def tables():
    l = np.arange(L)[:, None]
    k = np.arange(L)[None, :]
    ang = 2.0 * np.pi * ((l * k) % L) / L
    c, s = np.cos(ang), np.sin(ang)
    w_f = np.block([[c, -s], [s, c]])
    w_i = np.block([[c, s], [-s, c]])
    half = L // 2
    s_f = np.zeros((2 * L, 2 * L))
    s_i = np.zeros((2 * L, 2 * L))
    lo = np.arange(half)[None, :]
    hi = np.arange(half, L)[None, :]
    a0 = 2.0 * np.pi * ((l * lo) % L) / L
    a16 = 2.0 * np.pi * ((l * (16 + 32 * hi)) % N) / N
    s_f[:L, :half] = np.cos(a0)
    s_f[:L, L : L + half] = -np.sin(a0)
    s_f[:L, L] = 1.0 - 2.0 * (np.arange(L) % 2)
    s_f[L:, half:L] = np.cos(a16)
    s_f[L:, L + half :] = -np.sin(a16)
    s_i[:half, :L] = 2.0 * np.cos(a0).T
    s_i[L : L + half, :L] = -2.0 * np.sin(a0).T
    s_i[0, :L] = 1.0
    s_i[L, :L] = 1.0 - 2.0 * (np.arange(L) % 2)
    s_i[half:L, L:] = 2.0 * np.cos(a16).T
    s_i[L + half :, L:] = -2.0 * np.sin(a16).T
    mats = np.stack([_split_table(m) for m in (w_f, w_i, s_f.T, s_i)])
    q = np.arange(T)[:, None]
    tw = 2.0 * np.pi * ((q * np.arange(L)[None, :]) % N) / N
    return mats, np.stack([np.cos(tw), -np.sin(tw)]).astype(np.float32)


def slot_of(chunk, j):
    return PER * ((chunk + 1) % CHUNKS) + j


def times_w(re, im, k, n, sign):
    k %= n
    if k == 0:
        return re, im
    if 4 * k == n:
        return (-im, re) if sign > 0 else (im, -re)
    if 2 * k == n:
        return -re, -im
    r = math.sqrt(0.5)
    if 8 * k == n:
        return ((re - im) * r, (re + im) * r) if sign > 0 else ((re + im) * r, (im - re) * r)
    if 8 * k == 3 * n:
        return ((re + im) * -r, (re - im) * r) if sign > 0 else ((im - re) * r, (re + im) * -r)
    c = math.cos(2.0 * math.pi * k / n)
    s = sign * math.sin(2.0 * math.pi * k / n)
    return re * c - im * s, re * s + im * c


def cfft(vals, sign):
    n = len(vals)
    if n == 1:
        return vals
    even, odd = cfft(vals[0::2], sign), cfft(vals[1::2], sign)
    out = [None] * n
    for k in range(n // 2):
        a, b = even[k]
        c, d = times_w(*odd[k], k, n, sign)
        out[k] = (a + c, b + d)
        out[k + n // 2] = (a - c, b - d)
    return out


def rfft(vals):
    n = len(vals)
    if n == 2:
        return [(vals[0] + vals[1], None), (vals[0] - vals[1], None)]
    even, odd = rfft(vals[0::2]), rfft(vals[1::2])
    out = [None] * (n // 2 + 1)
    for k in range(n // 4 + 1):
        a, b = even[k]
        if k == 0:
            out[0] = (a + odd[0][0], None)
            out[n // 2] = (a - odd[0][0], None)
        elif k == n // 4:
            out[k] = (a, -odd[k][0])
        else:
            c, d = times_w(*odd[k], k, n, -1)
            out[k] = (a + c, b + d)
            out[n // 2 - k] = (a - c, d - b)
    return out


def irfft(bins):
    n = 2 * (len(bins) - 1)
    if n == 2:
        return [bins[0][0] + bins[1][0], bins[0][0] - bins[1][0]]
    even, odd = [None] * (n // 4 + 1), [None] * (n // 4 + 1)
    for k in range(n // 4 + 1):
        a, b = bins[k]
        if k == 0:
            c = bins[n // 2][0]
            even[0], odd[0] = (a + c, None), (a - c, None)
        elif k == n // 4:
            even[k], odd[k] = (2.0 * a, None), (-2.0 * b, None)
        else:
            c, d = bins[n // 2 - k]
            even[k] = (a + c, b - d)
            odd[k] = times_w(a - c, b + d, k, n, 1)
    out = [None] * n
    out[0::2], out[1::2] = irfft(even), irfft(odd)
    return out


def split(v):
    hi = v.astype(BF16)
    return hi, (v - hi.astype(F32)).astype(BF16)


def dot(a, b, nt=False):
    dims = (((1,), (1 if nt else 0,)), ((), ()))
    return lax.dot_general(a, b, dims, preferred_element_type=F32)


def dot3(data, mats, which):
    hi, lo = split(data)
    w_hi, w_lo = mats[which, 0], mats[which, 1]
    return dot(hi, w_hi) + (dot(lo, w_hi) + dot(hi, w_lo))


def field_kernel(
    off_hbm, x_hbm, amp_hbm, mats_hbm, tw_hbm,
    tx_out, ty_out, ratio_out,
    off, tw, mats, p_v, a_v, send1, recv1, send2, recv2, z_v, z2_v, amp_t, tmp_t, nyq, nyq_in, pr_v,
    up_s, low_s, sum_s, halo_s, halo_r, bs_main, in_main, gsel,
    x_sem, amp_sem, s1_sem, r1_sem, s2_sem, r2_sem, m_sem,
):
    gx, me = lax.axis_index("gx"), lax.axis_index("gy")
    north = lax.rem(me + G - 1, G)

    x_parts = [
        pltpu.make_async_copy(x_hbm.at[pl.ds(32 * i, 32)], p_v.at[pl.ds(32 * i, 32)], x_sem.at[i])
        for i in range(8)
    ]
    mats_cp = pltpu.make_async_copy(mats_hbm, mats, amp_sem.at[2])
    tw_cp = pltpu.make_async_copy(tw_hbm, tw, amp_sem.at[3])
    off_cp = pltpu.make_async_copy(off_hbm, off, amp_sem.at[4])
    tw_cp.start()
    for cp in x_parts:
        cp.start()

    barrier = pltpu.get_barrier_semaphore()
    for o in ORDER:
        pl.semaphore_signal(barrier, inc=1, device_id={"gy": lax.rem(me + o, G)}, device_id_type=MESH)
    for o in range(1, GX):
        pl.semaphore_signal(barrier, inc=1, device_id={"gx": lax.rem(gx + o, GX)}, device_id_type=MESH)
    mats_cp.start()
    off_cp.start()
    amp_parts = [
        pltpu.make_async_copy(amp_hbm.at[:, pl.ds(L * h, L)], pr_v.at[0, pl.ds(N * h, N)], amp_sem.at[h]) for h in range(2)
    ]
    for cp in amp_parts:
        cp.start()

    def x_tiles(i, carry):
        rows = pl.ds(pl.multiple_of(8 * i, 8), 8)
        bins = rfft([p_v[rows, L * t : L * (t + 1)] for t in range(T)])
        a_v[0, rows, :L] = bins[0][0]
        a_v[0, rows, L:] = bins[T // 2][0]
        for k in range(1, SLOTS):
            a, b = bins[k]
            c, s = tw[0, k : k + 1, :], tw[1, k : k + 1, :]
            a_v[k, rows, :L] = a * c - b * s
            a_v[k, rows, L:] = a * s + b * c
        return carry

    def first_refs(part, d):
        if part < 2:
            return send1.at[d, 0, part], recv1.at[0, me, part]
        return send1.at[d, part - 1], recv1.at[part - 1, me]

    def first_copy(part, o):
        d = lax.rem(me + o, G)
        src, dst = first_refs(part, d)
        return pltpu.make_async_remote_copy(
            src_ref=src, dst_ref=dst, send_sem=s1_sem.at[part, o], recv_sem=r1_sem.at[part, o],
            device_id={"gy": d}, device_id_type=MESH,
        )

    def first_own(part):
        src, dst = first_refs(part, me)
        return pltpu.make_async_copy(src, dst, r1_sem.at[part, 0])

    def send_first(part):
        for o in ORDER:
            first_copy(part, o).start()
        first_own(part).start()

    def second_refs(part, chunk, d):
        if part == 0:
            return send2.at[d, 0, chunk], recv2.at[0, chunk, me]
        pairs = pl.ds(PER // 2 * (part - 1), PER // 2)
        return send2.at[d, 1, chunk, pairs], recv2.at[1, chunk, me, pairs]

    def second_copy(part, chunk, o):
        d = lax.rem(me + o, G)
        src, dst = second_refs(part, chunk, d)
        return pltpu.make_async_remote_copy(
            src_ref=src, dst_ref=dst,
            send_sem=s2_sem.at[part, chunk, o], recv_sem=r2_sem.at[part, chunk, o],
            device_id={"gy": d}, device_id_type=MESH,
        )

    def second_own(part, chunk):
        src, dst = second_refs(part, chunk, me)
        return pltpu.make_async_copy(src, dst, r2_sem.at[part, chunk, 0])

    def send_second(part, chunk):
        for o in ORDER:
            second_copy(part, chunk, o).start()
        second_own(part, chunk).start()

    def x_lanes(j, carry, chunk, halves):
        slot = slot_of(chunk, j)
        which = jnp.where(slot == 0, 2, 1)
        data = a_v[slot] if len(halves) == 2 else a_v[slot, L * halves[0] : L * (halves[0] + 1), :]
        hi, lo = split(data)
        w_hi, w_lo = mats[which, 0], mats[which, 1]
        o = dot(w_hi, hi, True) + (dot(w_hi, lo, True) + dot(w_lo, hi, True))
        for n, h in enumerate(halves):
            for c in range(2):
                for d in range(G):
                    r = (c * G + d) * 8
                    send1[d, chunk, h, j, c] = o[r : r + 8, L * n : L * (n + 1)]
        return carry

    for h in range(2):
        for i in range(4 * h, 4 * h + 4):
            x_parts[i].wait()
            if i == 0:
                tw_cp.wait()
            lax.fori_loop(4 * i, 4 * i + 4, x_tiles, 0)
        if h == 0:
            mats_cp.wait()
            off_cp.wait()
        lax.fori_loop(0, PER, functools.partial(x_lanes, chunk=0, halves=(h,)), 0)
        if h == 0:
            pl.semaphore_wait(barrier, G - 1 + GX - 1)
        send_first(h)
    for chunk in range(1, CHUNKS):
        lax.fori_loop(0, PER, functools.partial(x_lanes, chunk=chunk, halves=(0, 1)), 0)
        send_first(chunk + 1)

    for cp in amp_parts:
        cp.wait()

    def amp_rows(q, carry):
        for h in range(2):
            block = pr_v[0, pl.ds(N * h + q, L, stride=T), :]
            tmp_t[L * h : L * (h + 1), :] = block.T
        first = jnp.where(me < G // 2, tmp_t[pl.ds(0, 8, stride=T), :], tmp_t[pl.ds(16, 8, stride=T), :])
        amp_t[q, 0:8, :] = first * (1.0 / (N * N))
        for k in range(1, SLOTS):
            amp_t[q, 8 * k : 8 * k + 8, :] = tmp_t[pl.ds(k, 8, stride=T), :] * (1.0 / (N * N))
        nyq[pl.ds(q, 1), :] = tmp_t[0:1, :] * (1.0 / (N * N))
        return carry

    lax.fori_loop(0, T, amp_rows, 0)
    nyq_cp = pltpu.make_async_remote_copy(
        src_ref=nyq, dst_ref=nyq_in, send_sem=m_sem.at[0], recv_sem=m_sem.at[1],
        device_id={"gy": 0}, device_id_type=MESH,
    )

    @pl.when(me == G // 2)
    def _():
        nyq_cp.start()
        nyq_cp.wait_send()


    shift_y, shift_x = off[0], off[1]
    wide = 1024 + L
    gsel[...] = jnp.where(
        (lax.broadcasted_iota(jnp.int32, (wide, L), 0) - shift_x) // 8
        == lax.broadcasted_iota(jnp.int32, (wide, L), 1),
        1.0,
        0.0,
    ).astype(BF16)

    lower = lax.broadcasted_iota(jnp.int32, (8, L), 1) < L // 2
    for chunk in range(CHUNKS):
        for part in (0, 1) if chunk == 0 else (chunk + 1,):
            for o in ORDER:
                first_copy(part, o).wait_recv()
            first_own(part).wait()

        def y_tiles(j, carry, chunk=chunk):
            rows = pl.ds(pl.multiple_of(8 * j, 8), 8)
            vals = [tuple(recv1[chunk, t // 2, t % 2, j, c] for c in range(2)) for t in range(T)]
            out = cfft(vals, -1)
            for q in range(T):
                a, b = out[q]
                if q > 0:
                    c, s = tw[0, q : q + 1, :], tw[1, q : q + 1, :]
                    a, b = a * c - b * s, a * s + b * c
                z_v[q, rows, :L] = a
                z_v[q, rows, L:] = b
            return carry

        lax.fori_loop(0, PER, y_tiles, 0)
        if chunk == CHUNKS - 1:

            @pl.when(me == 0)
            def _():
                nyq_cp.wait_recv()

        def y_lanes(b, carry, chunk=chunk):
            qs = pl.ds(8 * b, 8)
            f = dot3(z_v[qs].reshape(8 * 8 * PER, 2 * L), mats, 0)
            first = 8 * slot_of(chunk, 0)
            amp = amp_t[qs, first : first + 8 * PER, :].reshape(8 * 8 * PER, L)
            filtered = jnp.concatenate([f[:, :L] * amp, f[:, L:] * amp], axis=1)
            z_v[qs] = dot3(filtered, mats, 1).reshape(8, 8 * PER, 2 * L)
            if chunk == CHUNKS - 1:

                @pl.when(me == 0)
                def _():
                    other = nyq_in[qs]
                    other = jnp.broadcast_to(other[:, None, :], (8, 8, L)).reshape(64, L)
                    g = f.reshape(8, 8 * PER, 2 * L)[:, :8, :].reshape(64, 2 * L)
                    other = jnp.concatenate([g[:, :L] * other, g[:, L:] * other], axis=1)
                    z2_v[qs] = dot3(other, mats, 1).reshape(8, 8, 2 * L)

            return carry

        lax.fori_loop(0, T // 8, y_lanes, 0)

        def back(get):
            vals = []
            for q in range(T):
                a, b = get(q)
                if q > 0:
                    c, s = tw[0, q : q + 1, :], tw[1, q : q + 1, :]
                    a, b = a * c + b * s, b * c - a * s
                vals.append((a, b))
            return cfft(vals, 1)

        def y_back(j, carry, chunk=chunk):
            rows = pl.ds(pl.multiple_of(8 * j, 8), 8)
            out = back(lambda q: (z_v[q, rows, :L], z_v[q, rows, L:]))
            for t in range(T):
                for c in range(2):
                    send2[t // 2, t % 2, chunk, j, c] = out[t][c]
            return carry

        lax.fori_loop(0, PER, y_back, 0)
        if chunk == CHUNKS - 1:

            @pl.when(me == 0)
            def _():
                out = back(lambda q: (z2_v[q, :, :L], z2_v[q, :, L:]))
                for t in range(T):
                    send2[t // 2, t % 2, CHUNKS - 1, 0, 1, 0:1, :] = out[t][1][0:1, :]

        send_second(0, chunk)

        def pack(d, carry, chunk=chunk):
            for c in range(2):
                v = [send2[d, 1, chunk, j, c] for j in range(PER)]
                w = [pltpu.roll(one, L // 2, 1) for one in v]
                for n in range(PER // 2):
                    send2[d, 1, chunk, n, c] = jnp.where(lower, v[2 * n], w[2 * n + 1])
                    send2[d, 1, chunk, PER // 2 + n, c] = jnp.where(lower, w[2 * n], v[2 * n + 1])
            return carry

        lax.fori_loop(0, G, pack, 0)
    for part in range(1, 3):
        for chunk in range(CHUNKS):
            send_second(part, chunk)

    def put_back(slot, rows, o):
        a, b = o[:, :L], o[:, L:]
        c, s = tw[0, pl.ds(slot, 1), :], tw[1, pl.ds(slot, 1), :]
        a_v[slot, rows, :L] = a * c + b * s
        a_v[slot, rows, L:] = b * c - a * s

    def x_back(j, carry, chunk):
        slot = slot_of(chunk, j)
        data = jnp.concatenate(
            [recv2[0, chunk, d, j, c] for c in range(2) for d in range(G)], axis=0
        )
        put_back(slot, slice(0, L), dot3(data.T, mats, jnp.where(slot == 0, 3, 1)))
        return carry

    def x_back_pairs(part, chunk):
        half = L // 2
        rows = slice(L + half * (part - 1), L + half * part)
        for n in range(PER // 2):
            slot = slot_of(chunk, 2 * n)
            at = PER // 2 * (part - 1) + n
            data = jnp.concatenate(
                [recv2[1, chunk, d, at, c] for c in range(2) for d in range(G)], axis=0
            ).T
            o = dot3(data, mats, 1)
            put_back(slot, rows, dot3(data[:half], mats, 3) if slot == 0 else o[:half])
            put_back(slot + 1, rows, o[half:])

    def x_last(i, carry):
        rows = pl.ds(pl.multiple_of(8 * i, 8), 8)
        bins = [(a_v[0, rows, :L], None)]
        bins += [(a_v[k, rows, :L], a_v[k, rows, L:]) for k in range(1, SLOTS)]
        bins += [(a_v[0, rows, L:], None)]
        out = irfft(bins)
        for t in range(T):
            p = jnp.exp(out[t])
            p_v[rows, L * t : L * (t + 1)] = p
            here = pl.ds(pl.multiple_of(ROWS * t + 8 * i, 8), 8)
            pr_v[0, here, :] = p
            pr_v[1, here, :] = 1.0 / p
        return carry

    def y_sums(t, carry, first, count):
        for v in range(2):
            up, low = jnp.zeros((count, L), F32), jnp.zeros((count, L), F32)
            for a in range(8):
                u = pr_v[v, pl.ds(ROWS * t + 8 * first + a, count, stride=8), :]
                up += jnp.where(a >= shift_y, u, 0.0)
                low += jnp.where(a < shift_y, u, 0.0)
            up_s[v, t, first : first + count, :] = up
            low_s[v, t, first : first + count, :] = low
        return carry

    lane_end = lax.broadcasted_iota(jnp.int32, (8, L), 1) == L - 1

    def trans(i, carry):
        rows = pl.ds(pl.multiple_of(8 * i, 8), 8)
        after = pl.ds(pl.multiple_of(8 * i + 8, 8), 8)
        p = [p_v[rows, L * t : L * (t + 1)] for t in range(T)]
        rolled = [pltpu.roll(v, L - 1, 1) for v in p]
        for t in range(T):
            lanes = slice(L * t, L * (t + 1))
            q = jnp.where(lane_end, rolled[(t + 1) % T], rolled[t])
            tx_out[rows, lanes] = 2.0 * p[t] * q / (p[t] + q)
            q = jnp.concatenate([p[t], p_v[after, lanes]], axis=0)[1:9]
            ty_out[rows, lanes] = 2.0 * p[t] * q / (p[t] + q)
        return carry

    halo_cp = pltpu.make_async_remote_copy(
        src_ref=halo_s, dst_ref=halo_r, send_sem=m_sem.at[2], recv_sem=m_sem.at[3],
        device_id={"gy": north}, device_id_type=MESH,
    )
    def along_x(rows):
        parts = []
        for b in range(4):
            nxt = 1024 * (b + 1) % N
            lanes = [sum_s[rows, 1024 * b : 1024 * (b + 1)], sum_s[rows, nxt : nxt + L]]
            parts.append(jnp.concatenate(lanes, axis=1))
        data = jnp.concatenate(parts, axis=0)
        hi, lo = split(data)
        out = dot(jnp.concatenate([hi, lo], axis=0), gsel[...])
        out = out[: data.shape[0]] + out[data.shape[0] :]
        n = data.shape[0] // 4
        return [out[n * b : n * (b + 1)] for b in range(4)]

    last_row = lax.broadcasted_iota(jnp.int32, (T, L), 0) == T - 1
    for part, (first, count) in enumerate(((0, 16), (16, 8), (24, 8))):
        for chunk in range(CHUNKS):
            for o in ORDER:
                second_copy(part, chunk, o).wait_recv()
            second_own(part, chunk).wait()
            if part == 0:
                lax.fori_loop(0, PER, functools.partial(x_back, chunk=chunk), 0)
            else:
                x_back_pairs(part, chunk)
        lax.fori_loop(first, first + count, x_last, 0)
        lax.fori_loop(0, T, functools.partial(y_sums, first=first, count=count), 0)
        if part == 1:
            lax.fori_loop(15, 23, trans, 0)
        if part == 0:
            for t in range(T):
                halo_s[t : t + 1, :] = p_v[0:1, L * t : L * (t + 1)]
                for v in range(2):
                    sum_s[v : v + 1, L * t : L * (t + 1)] = low_s[v, t, 0:1, :]
            sum_s[2:8, :] = jnp.zeros((6, N), F32)
            for b, out in enumerate(along_x(slice(0, 8))):
                halo_s[T + 2 * b : T + 2 * b + 2, :] = out[0:2]
            halo_cp.start()
            lax.fori_loop(0, 15, trans, 0)

    for t in range(T):
        for v in range(2):
            moved = jnp.where(last_row, 0.0, pltpu.roll(low_s[v, t], T - 1, 0))
            sum_s[T * v : T * v + T, L * t : L * (t + 1)] = up_s[v, t] + moved
    halo_cp.wait()
    for b, out in enumerate(along_x(slice(0, 2 * T))):
        both = []
        for v in range(2):
            lead = jnp.broadcast_to(halo_r[T + 2 * b + v : T + 2 * b + v + 1, :], (T, L))
            both.append(out[T * v : T * v + T, :] + jnp.where(last_row, lead, 0.0))
        for h in range(2):
            mine = slice(L // 2 * h, L // 2 * (h + 1))
            bs_main[2 * b + h] = jnp.concatenate([v[:, mine] for v in both], axis=1)

    def main_copy(o):
        peer = lax.rem(gx + o, GX)
        return pltpu.make_async_remote_copy(
            src_ref=bs_main.at[peer], dst_ref=in_main.at[gx],
            send_sem=m_sem.at[8 + o], recv_sem=m_sem.at[16 + o],
            device_id={"gx": peer}, device_id_type=MESH,
        )

    own_main = pltpu.make_async_copy(bs_main.at[gx], in_main.at[gx], m_sem.at[16])
    own_main.start()
    for o in range(1, GX):
        main_copy(o).start()
    for t in range(T):
        p_v[ROWS : ROWS + 1, L * t : L * (t + 1)] = halo_r[t : t + 1, :]

    lax.fori_loop(23, 32, trans, 0)
    for part in range(CHUNKS + 1):
        for o in ORDER:
            first_copy(part, o).wait_send()
    for part in range(3):
        for chunk in range(CHUNKS):
            for o in ORDER:
                second_copy(part, chunk, o).wait_send()

    own_main.wait()
    for o in range(1, GX):
        main_copy(o).wait()
    sums = in_main[0]
    for g in range(1, GX):
        sums += in_main[g]
    ratio_out[...] = sums[:, : L // 2] / sums[:, L // 2 :]


def field(off, x, amp, mats, tw):
    hbm = pl.BlockSpec(memory_space=pltpu.HBM)
    vmem = pl.BlockSpec(memory_space=pltpu.VMEM)
    piece = (PER, 2, 8, L)
    return pl.pallas_call(
        field_kernel,
        out_shape=(
            jax.ShapeDtypeStruct((ROWS, N), F32),
            jax.ShapeDtypeStruct((ROWS, N), F32),
            jax.ShapeDtypeStruct((T, L // 2), F32),
        ),
        in_specs=[hbm] * 5,
        out_specs=(vmem, vmem, vmem),
        scratch_shapes=[
            pltpu.SMEM((2,), jnp.int32),
            pltpu.VMEM(tw.shape, F32),
            pltpu.VMEM(mats.shape, BF16),
            pltpu.VMEM((ROWS + 8, N), F32),
            pltpu.VMEM((SLOTS, ROWS, 2 * L), F32),
            pltpu.VMEM((G, CHUNKS, 2) + piece, F32),
            pltpu.VMEM((CHUNKS, G, 2) + piece, F32),
            pltpu.VMEM((G, 2, CHUNKS) + piece, F32),
            pltpu.VMEM((2, CHUNKS, G) + piece, F32),
            pltpu.VMEM((T, 8 * PER, 2 * L), F32),
            pltpu.VMEM((T, 8, 2 * L), F32),
            pltpu.VMEM((T, 8 * SLOTS, L), F32),
            pltpu.VMEM((2 * L + 16, L), F32),
            pltpu.VMEM((T, L), F32),
            pltpu.VMEM((T, L), F32),
            pltpu.VMEM((2, T * ROWS + 32, L), F32),
            pltpu.VMEM((2, T, T, L), F32),
            pltpu.VMEM((2, T, T, L), F32),
            pltpu.VMEM((2 * T, N), F32),
            pltpu.VMEM((T + 8, L), F32),
            pltpu.VMEM((T + 8, L), F32),
            pltpu.VMEM((GX, T, L), F32),
            pltpu.VMEM((GX, T, L), F32),
            pltpu.VMEM((1024 + L, L), BF16),
            pltpu.SemaphoreType.DMA((8,)),
            pltpu.SemaphoreType.DMA((5,)),
            pltpu.SemaphoreType.DMA((CHUNKS + 1, G)),
            pltpu.SemaphoreType.DMA((CHUNKS + 1, G)),
            pltpu.SemaphoreType.DMA((3, CHUNKS, G)),
            pltpu.SemaphoreType.DMA((3, CHUNKS, G)),
            pltpu.SemaphoreType.DMA((24,)),
        ],
        compiler_params=pltpu.CompilerParams(
            collective_id=0, has_side_effects=True, vmem_limit_bytes=44 << 20
        ),
        name="field",
    )(*(pltpu.with_memory_space_constraint(v, pltpu.HBM) for v in (off, x, amp, mats, tw)))


def write_kernel(tx, ty, ratio, tx_out, ty_out, up_out, sem):
    copies = []
    for n, (src, dst) in enumerate(((tx, tx_out), (ty, ty_out))):
        for i in range(4):
            rows = pl.ds(ROWS // 4 * i, ROWS // 4)
            copies.append(pltpu.make_async_copy(src.at[rows], dst.at[rows], sem.at[4 * n + i]))
    for cp in copies:
        cp.start()
    up_out[...] = jnp.sqrt(ratio[...])
    for cp in copies:
        cp.wait()


def written(tx, ty, ratio):
    hbm = pl.BlockSpec(memory_space=pltpu.HBM)
    vmem = pl.BlockSpec(memory_space=pltpu.VMEM)
    return pl.pallas_call(
        write_kernel,
        out_shape=(
            jax.ShapeDtypeStruct((ROWS, N), F32),
            jax.ShapeDtypeStruct((ROWS, N), F32),
            jax.ShapeDtypeStruct((T, L // 2), F32),
        ),
        in_specs=[pl.BlockSpec(memory_space=pl.ANY)] * 2 + [vmem],
        out_specs=(hbm, hbm, vmem),
        scratch_shapes=[pltpu.SemaphoreType.DMA((8,))],
        compiler_params=pltpu.CompilerParams(vmem_limit_bytes=1 << 20),
        name="write",
    )(tx, ty, ratio)


def shards(white_noise, amplitude, offsets):
    mats, tw = tables()
    tx, ty, ratio = field(offsets, white_noise[0], amplitude, jnp.asarray(mats), jnp.asarray(tw))
    trans_x, trans_y, upscaled = written(tx, ty, ratio)
    return trans_x[None], trans_y[None], upscaled


def solution(mesh):
    return jax.shard_map(
        shards,
        mesh=mesh,
        in_specs=(P("gx", "gy", None), P(None, "gy"), P()),
        out_specs=(P("gx", "gy", None), P("gx", "gy", None), P("gy", "gx")),
        check_vma=False,
    )
```

```python
import functools
import math

import jax
import jax.numpy as jnp
import numpy as np
from jax import lax
from jax.experimental import pallas as pl
from jax.experimental.pallas import tpu as pltpu
from jax.sharding import PartitionSpec as P

MESH = pl.DeviceIdType.MESH
F32 = jnp.float32
BF16 = jnp.bfloat16
L = 128
T = 32
N = L * T
SLOTS = 16
PER = 4
CHUNKS = SLOTS // PER
G = 16
GX = 8
ROWS = N // G
ORDER = [2, 4, 12, 14, 8, 6, 10, 3, 13, 5, 11, 9, 7, 15, 1]


def _split_table(m):
    hi = m.astype(jnp.bfloat16)
    lo = (m - hi.astype(np.float64)).astype(jnp.bfloat16)
    return np.stack([np.asarray(hi), np.asarray(lo)])


def tables():
    l = np.arange(L)[:, None]
    k = np.arange(L)[None, :]
    ang = 2.0 * np.pi * ((l * k) % L) / L
    c, s = np.cos(ang), np.sin(ang)
    w_f = np.block([[c, -s], [s, c]])
    w_i = np.block([[c, s], [-s, c]])
    half = L // 2
    s_f = np.zeros((2 * L, 2 * L))
    s_i = np.zeros((2 * L, 2 * L))
    lo = np.arange(half)[None, :]
    hi = np.arange(half, L)[None, :]
    a0 = 2.0 * np.pi * ((l * lo) % L) / L
    a16 = 2.0 * np.pi * ((l * (16 + 32 * hi)) % N) / N
    s_f[:L, :half] = np.cos(a0)
    s_f[:L, L : L + half] = -np.sin(a0)
    s_f[:L, L] = 1.0 - 2.0 * (np.arange(L) % 2)
    s_f[L:, half:L] = np.cos(a16)
    s_f[L:, L + half :] = -np.sin(a16)
    s_i[:half, :L] = 2.0 * np.cos(a0).T
    s_i[L : L + half, :L] = -2.0 * np.sin(a0).T
    s_i[0, :L] = 1.0
    s_i[L, :L] = 1.0 - 2.0 * (np.arange(L) % 2)
    s_i[half:L, L:] = 2.0 * np.cos(a16).T
    s_i[L + half :, L:] = -2.0 * np.sin(a16).T
    mats = np.stack([_split_table(m) for m in (w_f, w_i, s_f.T, s_i)])
    q = np.arange(T)[:, None]
    tw = 2.0 * np.pi * ((q * np.arange(L)[None, :]) % N) / N
    return mats, np.stack([np.cos(tw), -np.sin(tw)]).astype(np.float32)


def slot_of(chunk, j):
    return PER * ((chunk + 1) % CHUNKS) + j


def times_w(re, im, k, n, sign):
    k %= n
    if k == 0:
        return re, im
    if 4 * k == n:
        return (-im, re) if sign > 0 else (im, -re)
    if 2 * k == n:
        return -re, -im
    r = math.sqrt(0.5)
    if 8 * k == n:
        return ((re - im) * r, (re + im) * r) if sign > 0 else ((re + im) * r, (im - re) * r)
    if 8 * k == 3 * n:
        return ((re + im) * -r, (re - im) * r) if sign > 0 else ((im - re) * r, (re + im) * -r)
    c = math.cos(2.0 * math.pi * k / n)
    s = sign * math.sin(2.0 * math.pi * k / n)
    return re * c - im * s, re * s + im * c


def cfft(vals, sign):
    n = len(vals)
    if n == 1:
        return vals
    even, odd = cfft(vals[0::2], sign), cfft(vals[1::2], sign)
    out = [None] * n
    for k in range(n // 2):
        a, b = even[k]
        c, d = times_w(*odd[k], k, n, sign)
        out[k] = (a + c, b + d)
        out[k + n // 2] = (a - c, b - d)
    return out


def rfft(vals):
    n = len(vals)
    if n == 2:
        return [(vals[0] + vals[1], None), (vals[0] - vals[1], None)]
    even, odd = rfft(vals[0::2]), rfft(vals[1::2])
    out = [None] * (n // 2 + 1)
    for k in range(n // 4 + 1):
        a, b = even[k]
        if k == 0:
            out[0] = (a + odd[0][0], None)
            out[n // 2] = (a - odd[0][0], None)
        elif k == n // 4:
            out[k] = (a, -odd[k][0])
        else:
            c, d = times_w(*odd[k], k, n, -1)
            out[k] = (a + c, b + d)
            out[n // 2 - k] = (a - c, d - b)
    return out


def irfft(bins):
    n = 2 * (len(bins) - 1)
    if n == 2:
        return [bins[0][0] + bins[1][0], bins[0][0] - bins[1][0]]
    even, odd = [None] * (n // 4 + 1), [None] * (n // 4 + 1)
    for k in range(n // 4 + 1):
        a, b = bins[k]
        if k == 0:
            c = bins[n // 2][0]
            even[0], odd[0] = (a + c, None), (a - c, None)
        elif k == n // 4:
            even[k], odd[k] = (2.0 * a, None), (-2.0 * b, None)
        else:
            c, d = bins[n // 2 - k]
            even[k] = (a + c, b - d)
            odd[k] = times_w(a - c, b + d, k, n, 1)
    out = [None] * n
    out[0::2], out[1::2] = irfft(even), irfft(odd)
    return out


def split(v):
    hi = v.astype(BF16)
    return hi, (v - hi.astype(F32)).astype(BF16)


def dot(a, b, nt=False):
    dims = (((1,), (1 if nt else 0,)), ((), ()))
    return lax.dot_general(a, b, dims, preferred_element_type=F32)


def dot3(data, mats, which):
    hi, lo = split(data)
    w_hi, w_lo = mats[which, 0], mats[which, 1]
    return dot(hi, w_hi) + (dot(lo, w_hi) + dot(hi, w_lo))


def field_kernel(
    off_hbm, x_hbm, amp_hbm, mats_hbm, tw_hbm,
    tx_out, ty_out, ratio_out,
    off, tw, mats, p_v, a_v, send1, recv1, send2, recv2, z_v, z2_v, amp_t, tmp_t, nyq, nyq_in, pr_v,
    up_s, low_s, sum_s, halo_s, halo_r, bs_main, in_main, gsel,
    x_sem, amp_sem, s1_sem, r1_sem, s2_sem, r2_sem, m_sem,
):
    gx, me = lax.axis_index("gx"), lax.axis_index("gy")
    north = lax.rem(me + G - 1, G)

    x_parts = [
        pltpu.make_async_copy(x_hbm.at[pl.ds(32 * i, 32)], p_v.at[pl.ds(32 * i, 32)], x_sem.at[i])
        for i in range(8)
    ]
    mats_cp = pltpu.make_async_copy(mats_hbm, mats, amp_sem.at[2])
    tw_cp = pltpu.make_async_copy(tw_hbm, tw, amp_sem.at[3])
    off_cp = pltpu.make_async_copy(off_hbm, off, amp_sem.at[4])
    tw_cp.start()
    for cp in x_parts:
        cp.start()

    barrier = pltpu.get_barrier_semaphore()
    for o in ORDER:
        pl.semaphore_signal(barrier, inc=1, device_id={"gy": lax.rem(me + o, G)}, device_id_type=MESH)
    for o in range(1, GX):
        pl.semaphore_signal(barrier, inc=1, device_id={"gx": lax.rem(gx + o, GX)}, device_id_type=MESH)
    mats_cp.start()
    off_cp.start()
    amp_parts = [
        pltpu.make_async_copy(amp_hbm.at[:, pl.ds(L * h, L)], pr_v.at[0, pl.ds(N * h, N)], amp_sem.at[h]) for h in range(2)
    ]
    for cp in amp_parts:
        cp.start()

    def x_tiles(i, carry):
        rows = pl.ds(pl.multiple_of(8 * i, 8), 8)
        bins = rfft([p_v[rows, L * t : L * (t + 1)] for t in range(T)])
        a_v[0, rows, :L] = bins[0][0]
        a_v[0, rows, L:] = bins[T // 2][0]
        for k in range(1, SLOTS):
            a, b = bins[k]
            c, s = tw[0, k : k + 1, :], tw[1, k : k + 1, :]
            a_v[k, rows, :L] = a * c - b * s
            a_v[k, rows, L:] = a * s + b * c
        return carry

    def first_refs(part, d):
        if part < 2:
            return send1.at[d, 0, part], recv1.at[0, me, part]
        return send1.at[d, part - 1], recv1.at[part - 1, me]

    def first_copy(part, o):
        d = lax.rem(me + o, G)
        src, dst = first_refs(part, d)
        return pltpu.make_async_remote_copy(
            src_ref=src, dst_ref=dst, send_sem=s1_sem.at[part, o], recv_sem=r1_sem.at[part, o],
            device_id={"gy": d}, device_id_type=MESH,
        )

    def first_own(part):
        src, dst = first_refs(part, me)
        return pltpu.make_async_copy(src, dst, r1_sem.at[part, 0])

    def send_first(part):
        for o in ORDER:
            first_copy(part, o).start()
        first_own(part).start()

    def second_refs(part, chunk, d):
        if part == 0:
            return send2.at[d, 0, chunk], recv2.at[0, chunk, me]
        pairs = pl.ds(PER // 2 * (part - 1), PER // 2)
        return send2.at[d, 1, chunk, pairs], recv2.at[1, chunk, me, pairs]

    def second_copy(part, chunk, o):
        d = lax.rem(me + o, G)
        src, dst = second_refs(part, chunk, d)
        return pltpu.make_async_remote_copy(
            src_ref=src, dst_ref=dst,
            send_sem=s2_sem.at[part, chunk, o], recv_sem=r2_sem.at[part, chunk, o],
            device_id={"gy": d}, device_id_type=MESH,
        )

    def second_own(part, chunk):
        src, dst = second_refs(part, chunk, me)
        return pltpu.make_async_copy(src, dst, r2_sem.at[part, chunk, 0])

    def send_second(part, chunk):
        for o in ORDER:
            second_copy(part, chunk, o).start()
        second_own(part, chunk).start()

    def x_lanes(j, carry, chunk, halves):
        slot = slot_of(chunk, j)
        which = jnp.where(slot == 0, 2, 1)
        data = a_v[slot] if len(halves) == 2 else a_v[slot, L * halves[0] : L * (halves[0] + 1), :]
        hi, lo = split(data)
        w_hi, w_lo = mats[which, 0], mats[which, 1]
        o = dot(w_hi, hi, True) + (dot(w_hi, lo, True) + dot(w_lo, hi, True))
        for n, h in enumerate(halves):
            for c in range(2):
                for d in range(G):
                    r = (c * G + d) * 8
                    send1[d, chunk, h, j, c] = o[r : r + 8, L * n : L * (n + 1)]
        return carry

    for h in range(2):
        for i in range(4 * h, 4 * h + 4):
            x_parts[i].wait()
            if i == 0:
                tw_cp.wait()
            lax.fori_loop(4 * i, 4 * i + 4, x_tiles, 0, unroll=2)
        if h == 0:
            mats_cp.wait()
            off_cp.wait()
        lax.fori_loop(0, PER, functools.partial(x_lanes, chunk=0, halves=(h,)), 0, unroll=True)
        if h == 0:
            pl.semaphore_wait(barrier, G - 1 + GX - 1)
        send_first(h)
    for chunk in range(1, CHUNKS):
        lax.fori_loop(0, PER, functools.partial(x_lanes, chunk=chunk, halves=(0, 1)), 0)
        send_first(chunk + 1)

    for cp in amp_parts:
        cp.wait()

    def amp_rows(q, carry):
        for h in range(2):
            block = pr_v[0, pl.ds(N * h + q, L, stride=T), :]
            tmp_t[L * h : L * (h + 1), :] = block.T
        first = jnp.where(me < G // 2, tmp_t[pl.ds(0, 8, stride=T), :], tmp_t[pl.ds(16, 8, stride=T), :])
        amp_t[q, 0:8, :] = first * (1.0 / (N * N))
        for k in range(1, SLOTS):
            amp_t[q, 8 * k : 8 * k + 8, :] = tmp_t[pl.ds(k, 8, stride=T), :] * (1.0 / (N * N))
        nyq[pl.ds(q, 1), :] = tmp_t[0:1, :] * (1.0 / (N * N))
        return carry

    lax.fori_loop(0, T, amp_rows, 0)
    nyq_cp = pltpu.make_async_remote_copy(
        src_ref=nyq, dst_ref=nyq_in, send_sem=m_sem.at[0], recv_sem=m_sem.at[1],
        device_id={"gy": 0}, device_id_type=MESH,
    )

    @pl.when(me == G // 2)
    def _():
        nyq_cp.start()
        nyq_cp.wait_send()


    shift_y, shift_x = off[0], off[1]
    wide = 1024 + L
    gsel[...] = jnp.where(
        (lax.broadcasted_iota(jnp.int32, (wide, L), 0) - shift_x) // 8
        == lax.broadcasted_iota(jnp.int32, (wide, L), 1),
        1.0,
        0.0,
    ).astype(BF16)

    lower = lax.broadcasted_iota(jnp.int32, (8, L), 1) < L // 2
    for chunk in range(CHUNKS):
        for part in (0, 1) if chunk == 0 else (chunk + 1,):
            for o in ORDER:
                first_copy(part, o).wait_recv()
            first_own(part).wait()

        def y_tiles(j, carry, chunk=chunk):
            rows = pl.ds(pl.multiple_of(8 * j, 8), 8)
            vals = [tuple(recv1[chunk, t // 2, t % 2, j, c] for c in range(2)) for t in range(T)]
            out = cfft(vals, -1)
            for q in range(T):
                a, b = out[q]
                if q > 0:
                    c, s = tw[0, q : q + 1, :], tw[1, q : q + 1, :]
                    a, b = a * c - b * s, a * s + b * c
                z_v[q, rows, :L] = a
                z_v[q, rows, L:] = b
            return carry

        lax.fori_loop(0, PER, y_tiles, 0)
        if chunk == CHUNKS - 1:

            @pl.when(me == 0)
            def _():
                nyq_cp.wait_recv()

        def y_lanes(b, carry, chunk=chunk):
            qs = pl.ds(8 * b, 8)
            f = dot3(z_v[qs].reshape(8 * 8 * PER, 2 * L), mats, 0)
            first = 8 * slot_of(chunk, 0)
            amp = amp_t[qs, first : first + 8 * PER, :].reshape(8 * 8 * PER, L)
            filtered = jnp.concatenate([f[:, :L] * amp, f[:, L:] * amp], axis=1)
            z_v[qs] = dot3(filtered, mats, 1).reshape(8, 8 * PER, 2 * L)
            if chunk == CHUNKS - 1:

                @pl.when(me == 0)
                def _():
                    other = nyq_in[qs]
                    other = jnp.broadcast_to(other[:, None, :], (8, 8, L)).reshape(64, L)
                    g = f.reshape(8, 8 * PER, 2 * L)[:, :8, :].reshape(64, 2 * L)
                    other = jnp.concatenate([g[:, :L] * other, g[:, L:] * other], axis=1)
                    z2_v[qs] = dot3(other, mats, 1).reshape(8, 8, 2 * L)

            return carry

        lax.fori_loop(0, T // 8, y_lanes, 0)

        def back(get):
            vals = []
            for q in range(T):
                a, b = get(q)
                if q > 0:
                    c, s = tw[0, q : q + 1, :], tw[1, q : q + 1, :]
                    a, b = a * c + b * s, b * c - a * s
                vals.append((a, b))
            return cfft(vals, 1)

        def y_back(j, carry, chunk=chunk):
            rows = pl.ds(pl.multiple_of(8 * j, 8), 8)
            out = back(lambda q: (z_v[q, rows, :L], z_v[q, rows, L:]))
            for t in range(T):
                for c in range(2):
                    send2[t // 2, t % 2, chunk, j, c] = out[t][c]
            return carry

        lax.fori_loop(0, PER, y_back, 0)
        if chunk == CHUNKS - 1:

            @pl.when(me == 0)
            def _():
                out = back(lambda q: (z2_v[q, :, :L], z2_v[q, :, L:]))
                for t in range(T):
                    send2[t // 2, t % 2, CHUNKS - 1, 0, 1, 0:1, :] = out[t][1][0:1, :]

        send_second(0, chunk)

        def pack(d, carry, chunk=chunk):
            for c in range(2):
                v = [send2[d, 1, chunk, j, c] for j in range(PER)]
                w = [pltpu.roll(one, L // 2, 1) for one in v]
                for n in range(PER // 2):
                    send2[d, 1, chunk, n, c] = jnp.where(lower, v[2 * n], w[2 * n + 1])
                    send2[d, 1, chunk, PER // 2 + n, c] = jnp.where(lower, w[2 * n], v[2 * n + 1])
            return carry

        lax.fori_loop(0, G, pack, 0)
    for part in range(1, 3):
        for chunk in range(CHUNKS):
            send_second(part, chunk)
    for part in range(CHUNKS + 1):
        for o in ORDER:
            first_copy(part, o).wait_send()

    def sent(part):
        for chunk in range(CHUNKS):
            for o in ORDER:
                second_copy(part, chunk, o).wait_send()


    def put_back(slot, rows, o):
        a, b = o[:, :L], o[:, L:]
        c, s = tw[0, pl.ds(slot, 1), :], tw[1, pl.ds(slot, 1), :]
        a_v[slot, rows, :L] = a * c + b * s
        a_v[slot, rows, L:] = b * c - a * s

    def x_back(j, carry, chunk):
        slot = slot_of(chunk, j)
        data = jnp.concatenate(
            [recv2[0, chunk, d, j, c] for c in range(2) for d in range(G)], axis=0
        )
        put_back(slot, slice(0, L), dot3(data.T, mats, jnp.where(slot == 0, 3, 1)))
        return carry

    def x_back_pairs(part, chunk):
        half = L // 2
        rows = slice(L + half * (part - 1), L + half * part)
        for n in range(PER // 2):
            slot = slot_of(chunk, 2 * n)
            at = PER // 2 * (part - 1) + n
            data = jnp.concatenate(
                [recv2[1, chunk, d, at, c] for c in range(2) for d in range(G)], axis=0
            ).T
            o = dot3(data, mats, 1)
            put_back(slot, rows, dot3(data[:half], mats, 3) if slot == 0 else o[:half])
            put_back(slot + 1, rows, o[half:])

    def x_last(i, carry):
        rows = pl.ds(pl.multiple_of(8 * i, 8), 8)
        bins = [(a_v[0, rows, :L], None)]
        bins += [(a_v[k, rows, :L], a_v[k, rows, L:]) for k in range(1, SLOTS)]
        bins += [(a_v[0, rows, L:], None)]
        out = irfft(bins)
        for t in range(T):
            p = jnp.exp(out[t])
            p_v[rows, L * t : L * (t + 1)] = p
            here = pl.ds(pl.multiple_of(ROWS * t + 8 * i, 8), 8)
            pr_v[0, here, :] = p
            pr_v[1, here, :] = 1.0 / p
        return carry

    def y_sums(t, carry, first, count):
        for v in range(2):
            up, low = jnp.zeros((count, L), F32), jnp.zeros((count, L), F32)
            for a in range(8):
                u = pr_v[v, pl.ds(ROWS * t + 8 * first + a, count, stride=8), :]
                up += jnp.where(a >= shift_y, u, 0.0)
                low += jnp.where(a < shift_y, u, 0.0)
            up_s[v, t, first : first + count, :] = up
            low_s[v, t, first : first + count, :] = low
        return carry

    lane_end = lax.broadcasted_iota(jnp.int32, (8, L), 1) == L - 1

    def trans(i, carry):
        rows = pl.ds(pl.multiple_of(8 * i, 8), 8)
        after = pl.ds(pl.multiple_of(8 * i + 8, 8), 8)
        p = [p_v[rows, L * t : L * (t + 1)] for t in range(T)]
        rolled = [pltpu.roll(v, L - 1, 1) for v in p]
        for t in range(T):
            lanes = slice(L * t, L * (t + 1))
            q = jnp.where(lane_end, rolled[(t + 1) % T], rolled[t])
            tx_out[rows, lanes] = 2.0 * p[t] * q / (p[t] + q)
            q = jnp.concatenate([p[t], p_v[after, lanes]], axis=0)[1:9]
            ty_out[rows, lanes] = 2.0 * p[t] * q / (p[t] + q)
        return carry

    halo_cp = pltpu.make_async_remote_copy(
        src_ref=halo_s, dst_ref=halo_r, send_sem=m_sem.at[2], recv_sem=m_sem.at[3],
        device_id={"gy": north}, device_id_type=MESH,
    )
    def along_x(rows):
        parts = []
        for b in range(4):
            nxt = 1024 * (b + 1) % N
            lanes = [sum_s[rows, 1024 * b : 1024 * (b + 1)], sum_s[rows, nxt : nxt + L]]
            parts.append(jnp.concatenate(lanes, axis=1))
        data = jnp.concatenate(parts, axis=0)
        hi, lo = split(data)
        out = dot(jnp.concatenate([hi, lo], axis=0), gsel[...])
        out = out[: data.shape[0]] + out[data.shape[0] :]
        n = data.shape[0] // 4
        return [out[n * b : n * (b + 1)] for b in range(4)]

    last_row = lax.broadcasted_iota(jnp.int32, (T, L), 0) == T - 1
    for part, (first, count) in enumerate(((0, 16), (16, 8), (24, 8))):
        for chunk in range(CHUNKS):
            for o in ORDER:
                second_copy(part, chunk, o).wait_recv()
            second_own(part, chunk).wait()
            if part == 0:
                lax.fori_loop(0, PER, functools.partial(x_back, chunk=chunk), 0)
            else:
                x_back_pairs(part, chunk)
        lax.fori_loop(first, first + count, x_last, 0, unroll=2)
        lax.fori_loop(0, T, functools.partial(y_sums, first=first, count=count), 0, unroll=4)
        if part == 1:
            lax.fori_loop(15, 23, trans, 0)
            sent(1)
        if part == 0:
            for t in range(T):
                halo_s[t : t + 1, :] = p_v[0:1, L * t : L * (t + 1)]
                for v in range(2):
                    sum_s[v : v + 1, L * t : L * (t + 1)] = low_s[v, t, 0:1, :]
            sum_s[2:8, :] = jnp.zeros((6, N), F32)
            for b, out in enumerate(along_x(slice(0, 8))):
                halo_s[T + 2 * b : T + 2 * b + 2, :] = out[0:2]
            halo_cp.start()
            lax.fori_loop(0, 15, trans, 0)
            sent(0)

    for t in range(T):
        for v in range(2):
            moved = jnp.where(last_row, 0.0, pltpu.roll(low_s[v, t], T - 1, 0))
            sum_s[T * v : T * v + T, L * t : L * (t + 1)] = up_s[v, t] + moved
    halo_cp.wait()
    for b, out in enumerate(along_x(slice(0, 2 * T))):
        both = []
        for v in range(2):
            lead = jnp.broadcast_to(halo_r[T + 2 * b + v : T + 2 * b + v + 1, :], (T, L))
            both.append(out[T * v : T * v + T, :] + jnp.where(last_row, lead, 0.0))
        for h in range(2):
            mine = slice(L // 2 * h, L // 2 * (h + 1))
            bs_main[2 * b + h] = jnp.concatenate([v[:, mine] for v in both], axis=1)

    def main_copy(o):
        peer = lax.rem(gx + o, GX)
        return pltpu.make_async_remote_copy(
            src_ref=bs_main.at[peer], dst_ref=in_main.at[gx],
            send_sem=m_sem.at[8 + o], recv_sem=m_sem.at[16 + o],
            device_id={"gx": peer}, device_id_type=MESH,
        )

    own_main = pltpu.make_async_copy(bs_main.at[gx], in_main.at[gx], m_sem.at[16])
    own_main.start()
    for o in range(1, GX):
        main_copy(o).start()
    for t in range(T):
        p_v[ROWS : ROWS + 1, L * t : L * (t + 1)] = halo_r[t : t + 1, :]

    lax.fori_loop(23, 32, trans, 0)

    own_main.wait()
    for o in range(1, GX):
        main_copy(o).wait()
    sent(2)
    sums = in_main[0]
    for g in range(1, GX):
        sums += in_main[g]
    ratio_out[...] = sums[:, : L // 2] / sums[:, L // 2 :]


def field(off, x, amp, mats, tw):
    hbm = pl.BlockSpec(memory_space=pltpu.HBM)
    vmem = pl.BlockSpec(memory_space=pltpu.VMEM)
    piece = (PER, 2, 8, L)
    return pl.pallas_call(
        field_kernel,
        out_shape=(
            jax.ShapeDtypeStruct((ROWS, N), F32),
            jax.ShapeDtypeStruct((ROWS, N), F32),
            jax.ShapeDtypeStruct((T, L // 2), F32),
        ),
        in_specs=[hbm] * 5,
        out_specs=(vmem, vmem, vmem),
        scratch_shapes=[
            pltpu.SMEM((2,), jnp.int32),
            pltpu.VMEM(tw.shape, F32),
            pltpu.VMEM(mats.shape, BF16),
            pltpu.VMEM((ROWS + 8, N), F32),
            pltpu.VMEM((SLOTS, ROWS, 2 * L), F32),
            pltpu.VMEM((G, CHUNKS, 2) + piece, F32),
            pltpu.VMEM((CHUNKS, G, 2) + piece, F32),
            pltpu.VMEM((G, 2, CHUNKS) + piece, F32),
            pltpu.VMEM((2, CHUNKS, G) + piece, F32),
            pltpu.VMEM((T, 8 * PER, 2 * L), F32),
            pltpu.VMEM((T, 8, 2 * L), F32),
            pltpu.VMEM((T, 8 * SLOTS, L), F32),
            pltpu.VMEM((2 * L + 16, L), F32),
            pltpu.VMEM((T, L), F32),
            pltpu.VMEM((T, L), F32),
            pltpu.VMEM((2, T * ROWS + 32, L), F32),
            pltpu.VMEM((2, T, T, L), F32),
            pltpu.VMEM((2, T, T, L), F32),
            pltpu.VMEM((2 * T, N), F32),
            pltpu.VMEM((T + 8, L), F32),
            pltpu.VMEM((T + 8, L), F32),
            pltpu.VMEM((GX, T, L), F32),
            pltpu.VMEM((GX, T, L), F32),
            pltpu.VMEM((1024 + L, L), BF16),
            pltpu.SemaphoreType.DMA((8,)),
            pltpu.SemaphoreType.DMA((5,)),
            pltpu.SemaphoreType.DMA((CHUNKS + 1, G)),
            pltpu.SemaphoreType.DMA((CHUNKS + 1, G)),
            pltpu.SemaphoreType.DMA((3, CHUNKS, G)),
            pltpu.SemaphoreType.DMA((3, CHUNKS, G)),
            pltpu.SemaphoreType.DMA((24,)),
        ],
        compiler_params=pltpu.CompilerParams(
            collective_id=0, has_side_effects=True, vmem_limit_bytes=44 << 20
        ),
        name="field",
    )(*(pltpu.with_memory_space_constraint(v, pltpu.HBM) for v in (off, x, amp, mats, tw)))


def write_kernel(tx, ty, ratio, tx_out, ty_out, up_out, sem):
    copies = []
    for n, (src, dst) in enumerate(((tx, tx_out), (ty, ty_out))):
        for i in range(4):
            rows = pl.ds(ROWS // 4 * i, ROWS // 4)
            copies.append(pltpu.make_async_copy(src.at[rows], dst.at[rows], sem.at[4 * n + i]))
    for cp in copies:
        cp.start()
    up_out[...] = jnp.sqrt(ratio[...])
    for cp in copies:
        cp.wait()


def written(tx, ty, ratio):
    hbm = pl.BlockSpec(memory_space=pltpu.HBM)
    vmem = pl.BlockSpec(memory_space=pltpu.VMEM)
    return pl.pallas_call(
        write_kernel,
        out_shape=(
            jax.ShapeDtypeStruct((ROWS, N), F32),
            jax.ShapeDtypeStruct((ROWS, N), F32),
            jax.ShapeDtypeStruct((T, L // 2), F32),
        ),
        in_specs=[pl.BlockSpec(memory_space=pl.ANY)] * 2 + [vmem],
        out_specs=(hbm, hbm, vmem),
        scratch_shapes=[pltpu.SemaphoreType.DMA((8,))],
        compiler_params=pltpu.CompilerParams(vmem_limit_bytes=1 << 20),
        name="write",
    )(tx, ty, ratio)


def shards(white_noise, amplitude, offsets):
    mats, tw = tables()
    tx, ty, ratio = field(offsets, white_noise[0], amplitude, jnp.asarray(mats), jnp.asarray(tw))
    trans_x, trans_y, upscaled = written(tx, ty, ratio)
    return trans_x[None], trans_y[None], upscaled


def solution(mesh):
    return jax.shard_map(
        shards,
        mesh=mesh,
        in_specs=(P("gx", "gy", None), P(None, "gy"), P()),
        out_specs=(P("gx", "gy", None), P("gx", "gy", None), P("gy", "gx")),
        check_vma=False,
    )
```

```python
import functools
import math

import jax
import jax.numpy as jnp
import numpy as np
from jax import lax
from jax.experimental import pallas as pl
from jax.experimental.pallas import tpu as pltpu
from jax.sharding import PartitionSpec as P

MESH = pl.DeviceIdType.MESH
F32 = jnp.float32
BF16 = jnp.bfloat16
L = 128
T = 32
N = L * T
SLOTS = 16
PER = 4
CHUNKS = SLOTS // PER
G = 16
GX = 8
ROWS = N // G
ORDER = [2, 4, 12, 14, 8, 6, 10, 3, 13, 5, 11, 9, 7, 15, 1]


def _split_table(m):
    hi = m.astype(jnp.bfloat16)
    lo = (m - hi.astype(np.float64)).astype(jnp.bfloat16)
    return np.stack([np.asarray(hi), np.asarray(lo)])


def tables():
    l = np.arange(L)[:, None]
    k = np.arange(L)[None, :]
    ang = 2.0 * np.pi * ((l * k) % L) / L
    c, s = np.cos(ang), np.sin(ang)
    w_f = np.block([[c, -s], [s, c]])
    w_i = np.block([[c, s], [-s, c]])
    half = L // 2
    s_f = np.zeros((2 * L, 2 * L))
    s_i = np.zeros((2 * L, 2 * L))
    lo = np.arange(half)[None, :]
    hi = np.arange(half, L)[None, :]
    a0 = 2.0 * np.pi * ((l * lo) % L) / L
    a16 = 2.0 * np.pi * ((l * (16 + 32 * hi)) % N) / N
    s_f[:L, :half] = np.cos(a0)
    s_f[:L, L : L + half] = -np.sin(a0)
    s_f[:L, L] = 1.0 - 2.0 * (np.arange(L) % 2)
    s_f[L:, half:L] = np.cos(a16)
    s_f[L:, L + half :] = -np.sin(a16)
    s_i[:half, :L] = 2.0 * np.cos(a0).T
    s_i[L : L + half, :L] = -2.0 * np.sin(a0).T
    s_i[0, :L] = 1.0
    s_i[L, :L] = 1.0 - 2.0 * (np.arange(L) % 2)
    s_i[half:L, L:] = 2.0 * np.cos(a16).T
    s_i[L + half :, L:] = -2.0 * np.sin(a16).T
    mats = np.stack([_split_table(m) for m in (w_f, w_i, s_f.T, s_i)])
    q = np.arange(T)[:, None]
    tw = 2.0 * np.pi * ((q * np.arange(L)[None, :]) % N) / N
    return mats, np.stack([np.cos(tw), -np.sin(tw)]).astype(np.float32)


def slot_of(chunk, j):
    return PER * ((chunk + 1) % CHUNKS) + j


def times_w(re, im, k, n, sign):
    k %= n
    if k == 0:
        return re, im
    if 4 * k == n:
        return (-im, re) if sign > 0 else (im, -re)
    if 2 * k == n:
        return -re, -im
    r = math.sqrt(0.5)
    if 8 * k == n:
        return ((re - im) * r, (re + im) * r) if sign > 0 else ((re + im) * r, (im - re) * r)
    if 8 * k == 3 * n:
        return ((re + im) * -r, (re - im) * r) if sign > 0 else ((im - re) * r, (re + im) * -r)
    c = math.cos(2.0 * math.pi * k / n)
    s = sign * math.sin(2.0 * math.pi * k / n)
    return re * c - im * s, re * s + im * c


def cfft(vals, sign):
    n = len(vals)
    if n == 1:
        return vals
    even, odd = cfft(vals[0::2], sign), cfft(vals[1::2], sign)
    out = [None] * n
    for k in range(n // 2):
        a, b = even[k]
        c, d = times_w(*odd[k], k, n, sign)
        out[k] = (a + c, b + d)
        out[k + n // 2] = (a - c, b - d)
    return out


def rfft(vals):
    n = len(vals)
    if n == 2:
        return [(vals[0] + vals[1], None), (vals[0] - vals[1], None)]
    even, odd = rfft(vals[0::2]), rfft(vals[1::2])
    out = [None] * (n // 2 + 1)
    for k in range(n // 4 + 1):
        a, b = even[k]
        if k == 0:
            out[0] = (a + odd[0][0], None)
            out[n // 2] = (a - odd[0][0], None)
        elif k == n // 4:
            out[k] = (a, -odd[k][0])
        else:
            c, d = times_w(*odd[k], k, n, -1)
            out[k] = (a + c, b + d)
            out[n // 2 - k] = (a - c, d - b)
    return out


def irfft(bins):
    n = 2 * (len(bins) - 1)
    if n == 2:
        return [bins[0][0] + bins[1][0], bins[0][0] - bins[1][0]]
    even, odd = [None] * (n // 4 + 1), [None] * (n // 4 + 1)
    for k in range(n // 4 + 1):
        a, b = bins[k]
        if k == 0:
            c = bins[n // 2][0]
            even[0], odd[0] = (a + c, None), (a - c, None)
        elif k == n // 4:
            even[k], odd[k] = (2.0 * a, None), (-2.0 * b, None)
        else:
            c, d = bins[n // 2 - k]
            even[k] = (a + c, b - d)
            odd[k] = times_w(a - c, b + d, k, n, 1)
    out = [None] * n
    out[0::2], out[1::2] = irfft(even), irfft(odd)
    return out


def split(v):
    hi = v.astype(BF16)
    return hi, (v - hi.astype(F32)).astype(BF16)


def dot(a, b, nt=False):
    dims = (((1,), (1 if nt else 0,)), ((), ()))
    return lax.dot_general(a, b, dims, preferred_element_type=F32)


def dot3(data, mats, which):
    hi, lo = split(data)
    w_hi, w_lo = mats[which, 0], mats[which, 1]
    return dot(hi, w_hi) + (dot(lo, w_hi) + dot(hi, w_lo))


def field_kernel(
    off_hbm, x_hbm, amp_hbm, mats_hbm, tw_hbm,
    tx_out, ty_out, sums_out,
    off, tw, mats, p_v, a_v, send1, recv1, send2, recv2, z_v, z2_v, amp_t, tmp_t, nyq, nyq_in, pr_v,
    up_s, low_s, sum_s, halo_s, halo_r, bs_main, in_main, gsel,
    x_sem, amp_sem, s1_sem, r1_sem, s2_sem, r2_sem, m_sem,
):
    gx, me = lax.axis_index("gx"), lax.axis_index("gy")
    north = lax.rem(me + G - 1, G)

    x_parts = [
        pltpu.make_async_copy(x_hbm.at[pl.ds(32 * i, 32)], p_v.at[pl.ds(32 * i, 32)], x_sem.at[i])
        for i in range(8)
    ]
    mats_cp = pltpu.make_async_copy(mats_hbm, mats, amp_sem.at[2])
    tw_cp = pltpu.make_async_copy(tw_hbm, tw, amp_sem.at[3])
    off_cp = pltpu.make_async_copy(off_hbm, off, amp_sem.at[4])
    tw_cp.start()
    for cp in x_parts:
        cp.start()

    barrier = pltpu.get_barrier_semaphore()
    for o in ORDER:
        pl.semaphore_signal(barrier, inc=1, device_id={"gy": lax.rem(me + o, G)}, device_id_type=MESH)
    for o in range(1, GX):
        pl.semaphore_signal(barrier, inc=1, device_id={"gx": lax.rem(gx + o, GX)}, device_id_type=MESH)
    mats_cp.start()
    off_cp.start()
    amp_parts = [
        pltpu.make_async_copy(amp_hbm.at[:, pl.ds(L * h, L)], pr_v.at[0, pl.ds(N * h, N)], amp_sem.at[h]) for h in range(2)
    ]
    for cp in amp_parts:
        cp.start()

    def x_tiles(i, carry):
        rows = pl.ds(pl.multiple_of(8 * i, 8), 8)
        bins = rfft([p_v[rows, L * t : L * (t + 1)] for t in range(T)])
        a_v[0, rows, :L] = bins[0][0]
        a_v[0, rows, L:] = bins[T // 2][0]
        for k in range(1, SLOTS):
            a, b = bins[k]
            c, s = tw[0, k : k + 1, :], tw[1, k : k + 1, :]
            a_v[k, rows, :L] = a * c - b * s
            a_v[k, rows, L:] = a * s + b * c
        return carry

    def first_refs(part, d):
        if part < 2:
            return send1.at[d, 0, part], recv1.at[0, me, part]
        return send1.at[d, part - 1], recv1.at[part - 1, me]

    def first_copy(part, o):
        d = lax.rem(me + o, G)
        src, dst = first_refs(part, d)
        return pltpu.make_async_remote_copy(
            src_ref=src, dst_ref=dst, send_sem=s1_sem.at[part, o], recv_sem=r1_sem.at[part, o],
            device_id={"gy": d}, device_id_type=MESH,
        )

    def first_own(part):
        src, dst = first_refs(part, me)
        return pltpu.make_async_copy(src, dst, r1_sem.at[part, 0])

    def send_first(part):
        for o in ORDER:
            first_copy(part, o).start()
        first_own(part).start()

    def second_refs(part, chunk, d):
        if part == 0:
            return send2.at[d, 0, chunk], recv2.at[0, chunk, me]
        pairs = pl.ds(PER // 2 * (part - 1), PER // 2)
        return send2.at[d, 1, chunk, pairs], recv2.at[1, chunk, me, pairs]

    def second_copy(part, chunk, o):
        d = lax.rem(me + o, G)
        src, dst = second_refs(part, chunk, d)
        return pltpu.make_async_remote_copy(
            src_ref=src, dst_ref=dst,
            send_sem=s2_sem.at[part, chunk, o], recv_sem=r2_sem.at[part, chunk, o],
            device_id={"gy": d}, device_id_type=MESH,
        )

    def second_own(part, chunk):
        src, dst = second_refs(part, chunk, me)
        return pltpu.make_async_copy(src, dst, r2_sem.at[part, chunk, 0])

    def send_second(part, chunk):
        for o in ORDER:
            second_copy(part, chunk, o).start()
        second_own(part, chunk).start()

    def x_lanes(j, carry, chunk, halves):
        slot = slot_of(chunk, j)
        which = jnp.where(slot == 0, 2, 1)
        data = a_v[slot] if len(halves) == 2 else a_v[slot, L * halves[0] : L * (halves[0] + 1), :]
        hi, lo = split(data)
        w_hi, w_lo = mats[which, 0], mats[which, 1]
        o = dot(w_hi, hi, True) + (dot(w_hi, lo, True) + dot(w_lo, hi, True))
        for n, h in enumerate(halves):
            for c in range(2):
                for d in range(G):
                    r = (c * G + d) * 8
                    send1[d, chunk, h, j, c] = o[r : r + 8, L * n : L * (n + 1)]
        return carry

    for h in range(2):
        for i in range(4 * h, 4 * h + 4):
            x_parts[i].wait()
            if i == 0:
                tw_cp.wait()
            lax.fori_loop(4 * i, 4 * i + 4, x_tiles, 0, unroll=2)
        if h == 0:
            mats_cp.wait()
            off_cp.wait()
        lax.fori_loop(0, PER, functools.partial(x_lanes, chunk=0, halves=(h,)), 0, unroll=True)
        if h == 0:
            pl.semaphore_wait(barrier, G - 1 + GX - 1)
        send_first(h)
    for chunk in range(1, CHUNKS):
        lax.fori_loop(0, PER, functools.partial(x_lanes, chunk=chunk, halves=(0, 1)), 0)
        send_first(chunk + 1)

    for cp in amp_parts:
        cp.wait()

    def amp_rows(q, carry):
        for h in range(2):
            block = pr_v[0, pl.ds(N * h + q, L, stride=T), :]
            tmp_t[L * h : L * (h + 1), :] = block.T
        first = jnp.where(me < G // 2, tmp_t[pl.ds(0, 8, stride=T), :], tmp_t[pl.ds(16, 8, stride=T), :])
        amp_t[q, 0:8, :] = first * (1.0 / (N * N))
        for k in range(1, SLOTS):
            amp_t[q, 8 * k : 8 * k + 8, :] = tmp_t[pl.ds(k, 8, stride=T), :] * (1.0 / (N * N))
        nyq[pl.ds(q, 1), :] = tmp_t[0:1, :] * (1.0 / (N * N))
        return carry

    lax.fori_loop(0, T, amp_rows, 0)
    nyq_cp = pltpu.make_async_remote_copy(
        src_ref=nyq, dst_ref=nyq_in, send_sem=m_sem.at[0], recv_sem=m_sem.at[1],
        device_id={"gy": 0}, device_id_type=MESH,
    )

    @pl.when(me == G // 2)
    def _():
        nyq_cp.start()
        nyq_cp.wait_send()


    shift_y, shift_x = off[0], off[1]
    wide = 1024 + L
    gsel[...] = jnp.where(
        (lax.broadcasted_iota(jnp.int32, (wide, L), 0) - shift_x) // 8
        == lax.broadcasted_iota(jnp.int32, (wide, L), 1),
        1.0,
        0.0,
    ).astype(BF16)

    lower = lax.broadcasted_iota(jnp.int32, (8, L), 1) < L // 2
    for chunk in range(CHUNKS):
        for part in (0, 1) if chunk == 0 else (chunk + 1,):
            for o in ORDER:
                first_copy(part, o).wait_recv()
            first_own(part).wait()

        def y_tiles(j, carry, chunk=chunk):
            rows = pl.ds(pl.multiple_of(8 * j, 8), 8)
            vals = [tuple(recv1[chunk, t // 2, t % 2, j, c] for c in range(2)) for t in range(T)]
            out = cfft(vals, -1)
            for q in range(T):
                a, b = out[q]
                if q > 0:
                    c, s = tw[0, q : q + 1, :], tw[1, q : q + 1, :]
                    a, b = a * c - b * s, a * s + b * c
                z_v[q, rows, :L] = a
                z_v[q, rows, L:] = b
            return carry

        lax.fori_loop(0, PER, y_tiles, 0)
        if chunk == CHUNKS - 1:

            @pl.when(me == 0)
            def _():
                nyq_cp.wait_recv()

        def y_lanes(b, carry, chunk=chunk):
            qs = pl.ds(8 * b, 8)
            f = dot3(z_v[qs].reshape(8 * 8 * PER, 2 * L), mats, 0)
            first = 8 * slot_of(chunk, 0)
            amp = amp_t[qs, first : first + 8 * PER, :].reshape(8 * 8 * PER, L)
            filtered = jnp.concatenate([f[:, :L] * amp, f[:, L:] * amp], axis=1)
            z_v[qs] = dot3(filtered, mats, 1).reshape(8, 8 * PER, 2 * L)
            if chunk == CHUNKS - 1:

                @pl.when(me == 0)
                def _():
                    other = nyq_in[qs]
                    other = jnp.broadcast_to(other[:, None, :], (8, 8, L)).reshape(64, L)
                    g = f.reshape(8, 8 * PER, 2 * L)[:, :8, :].reshape(64, 2 * L)
                    other = jnp.concatenate([g[:, :L] * other, g[:, L:] * other], axis=1)
                    z2_v[qs] = dot3(other, mats, 1).reshape(8, 8, 2 * L)

            return carry

        lax.fori_loop(0, T // 8, y_lanes, 0)

        def back(get):
            vals = []
            for q in range(T):
                a, b = get(q)
                if q > 0:
                    c, s = tw[0, q : q + 1, :], tw[1, q : q + 1, :]
                    a, b = a * c + b * s, b * c - a * s
                vals.append((a, b))
            return cfft(vals, 1)

        def y_back(j, carry, chunk=chunk):
            rows = pl.ds(pl.multiple_of(8 * j, 8), 8)
            out = back(lambda q: (z_v[q, rows, :L], z_v[q, rows, L:]))
            for t in range(T):
                for c in range(2):
                    send2[t // 2, t % 2, chunk, j, c] = out[t][c]
            return carry

        lax.fori_loop(0, PER, y_back, 0)
        if chunk == CHUNKS - 1:

            @pl.when(me == 0)
            def _():
                out = back(lambda q: (z2_v[q, :, :L], z2_v[q, :, L:]))
                for t in range(T):
                    send2[t // 2, t % 2, CHUNKS - 1, 0, 1, 0:1, :] = out[t][1][0:1, :]

        send_second(0, chunk)

        def pack(d, carry, chunk=chunk):
            for c in range(2):
                v = [send2[d, 1, chunk, j, c] for j in range(PER)]
                w = [pltpu.roll(one, L // 2, 1) for one in v]
                for n in range(PER // 2):
                    send2[d, 1, chunk, n, c] = jnp.where(lower, v[2 * n], w[2 * n + 1])
                    send2[d, 1, chunk, PER // 2 + n, c] = jnp.where(lower, w[2 * n], v[2 * n + 1])
            return carry

        lax.fori_loop(0, G, pack, 0)
    for part in range(1, 3):
        for chunk in range(CHUNKS):
            send_second(part, chunk)
    for part in range(CHUNKS + 1):
        for o in ORDER:
            first_copy(part, o).wait_send()

    def sent(part):
        for chunk in range(CHUNKS):
            for o in ORDER:
                second_copy(part, chunk, o).wait_send()


    def put_back(slot, rows, o):
        a, b = o[:, :L], o[:, L:]
        c, s = tw[0, pl.ds(slot, 1), :], tw[1, pl.ds(slot, 1), :]
        a_v[slot, rows, :L] = a * c + b * s
        a_v[slot, rows, L:] = b * c - a * s

    def x_back(j, carry, chunk):
        slot = slot_of(chunk, j)
        data = jnp.concatenate(
            [recv2[0, chunk, d, j, c] for c in range(2) for d in range(G)], axis=0
        )
        put_back(slot, slice(0, L), dot3(data.T, mats, jnp.where(slot == 0, 3, 1)))
        return carry

    def x_back_pairs(part, chunk):
        half = L // 2
        rows = slice(L + half * (part - 1), L + half * part)
        for n in range(PER // 2):
            slot = slot_of(chunk, 2 * n)
            at = PER // 2 * (part - 1) + n
            data = jnp.concatenate(
                [recv2[1, chunk, d, at, c] for c in range(2) for d in range(G)], axis=0
            ).T
            o = dot3(data, mats, 1)
            put_back(slot, rows, dot3(data[:half], mats, 3) if slot == 0 else o[:half])
            put_back(slot + 1, rows, o[half:])

    def x_last(i, carry):
        rows = pl.ds(pl.multiple_of(8 * i, 8), 8)
        bins = [(a_v[0, rows, :L], None)]
        bins += [(a_v[k, rows, :L], a_v[k, rows, L:]) for k in range(1, SLOTS)]
        bins += [(a_v[0, rows, L:], None)]
        out = irfft(bins)
        for t in range(T):
            p = jnp.exp(out[t])
            p_v[rows, L * t : L * (t + 1)] = p
            here = pl.ds(pl.multiple_of(ROWS * t + 8 * i, 8), 8)
            pr_v[0, here, :] = p
            pr_v[1, here, :] = 1.0 / p
        return carry

    def y_sums(t, carry, first, count):
        for v in range(2):
            up, low = jnp.zeros((count, L), F32), jnp.zeros((count, L), F32)
            for a in range(8):
                u = pr_v[v, pl.ds(ROWS * t + 8 * first + a, count, stride=8), :]
                up += jnp.where(a >= shift_y, u, 0.0)
                low += jnp.where(a < shift_y, u, 0.0)
            up_s[v, t, first : first + count, :] = up
            low_s[v, t, first : first + count, :] = low
        return carry

    lane_end = lax.broadcasted_iota(jnp.int32, (8, L), 1) == L - 1

    def trans(i, carry):
        rows = pl.ds(pl.multiple_of(8 * i, 8), 8)
        after = pl.ds(pl.multiple_of(8 * i + 8, 8), 8)
        p = [p_v[rows, L * t : L * (t + 1)] for t in range(T)]
        rolled = [pltpu.roll(v, L - 1, 1) for v in p]
        for t in range(T):
            lanes = slice(L * t, L * (t + 1))
            q = jnp.where(lane_end, rolled[(t + 1) % T], rolled[t])
            tx_out[rows, lanes] = 2.0 * p[t] * q / (p[t] + q)
            q = jnp.concatenate([p[t], p_v[after, lanes]], axis=0)[1:9]
            ty_out[rows, lanes] = 2.0 * p[t] * q / (p[t] + q)
        return carry

    halo_cp = pltpu.make_async_remote_copy(
        src_ref=halo_s, dst_ref=halo_r, send_sem=m_sem.at[2], recv_sem=m_sem.at[3],
        device_id={"gy": north}, device_id_type=MESH,
    )
    def along_x(rows):
        parts = []
        for b in range(4):
            nxt = 1024 * (b + 1) % N
            lanes = [sum_s[rows, 1024 * b : 1024 * (b + 1)], sum_s[rows, nxt : nxt + L]]
            parts.append(jnp.concatenate(lanes, axis=1))
        data = jnp.concatenate(parts, axis=0)
        hi, lo = split(data)
        out = dot(jnp.concatenate([hi, lo], axis=0), gsel[...])
        out = out[: data.shape[0]] + out[data.shape[0] :]
        n = data.shape[0] // 4
        return [out[n * b : n * (b + 1)] for b in range(4)]

    last_row = lax.broadcasted_iota(jnp.int32, (T, L), 0) == T - 1
    for part, (first, count) in enumerate(((0, 16), (16, 8), (24, 8))):
        for chunk in range(CHUNKS):
            for o in ORDER:
                second_copy(part, chunk, o).wait_recv()
            second_own(part, chunk).wait()
            if part == 0:
                lax.fori_loop(0, PER, functools.partial(x_back, chunk=chunk), 0)
            else:
                x_back_pairs(part, chunk)
        lax.fori_loop(first, first + count, x_last, 0, unroll=2)
        lax.fori_loop(0, T, functools.partial(y_sums, first=first, count=count), 0, unroll=8)
        if part == 1:
            lax.fori_loop(15, 23, trans, 0)
            sent(1)
        if part == 0:
            for t in range(T):
                halo_s[t : t + 1, :] = p_v[0:1, L * t : L * (t + 1)]
                for v in range(2):
                    sum_s[v : v + 1, L * t : L * (t + 1)] = low_s[v, t, 0:1, :]
            sum_s[2:8, :] = jnp.zeros((6, N), F32)
            for b, out in enumerate(along_x(slice(0, 8))):
                halo_s[T + 2 * b : T + 2 * b + 2, :] = out[0:2]
            halo_cp.start()
            lax.fori_loop(0, 15, trans, 0)
            sent(0)

    for t in range(T):
        for v in range(2):
            moved = jnp.where(last_row, 0.0, pltpu.roll(low_s[v, t], T - 1, 0))
            sum_s[T * v : T * v + T, L * t : L * (t + 1)] = up_s[v, t] + moved
    halo_cp.wait()
    for b, out in enumerate(along_x(slice(0, 2 * T))):
        both = []
        for v in range(2):
            lead = jnp.broadcast_to(halo_r[T + 2 * b + v : T + 2 * b + v + 1, :], (T, L))
            both.append(out[T * v : T * v + T, :] + jnp.where(last_row, lead, 0.0))
        for h in range(2):
            mine = slice(L // 2 * h, L // 2 * (h + 1))
            bs_main[2 * b + h] = jnp.concatenate([v[:, mine] for v in both], axis=1)

    def main_copy(o):
        peer = lax.rem(gx + o, GX)
        return pltpu.make_async_remote_copy(
            src_ref=bs_main.at[peer], dst_ref=in_main.at[gx],
            send_sem=m_sem.at[8 + o], recv_sem=m_sem.at[16 + o],
            device_id={"gx": peer}, device_id_type=MESH,
        )

    own_main = pltpu.make_async_copy(bs_main.at[gx], in_main.at[gx], m_sem.at[16])
    own_main.start()
    for o in range(1, GX):
        main_copy(o).start()
    for t in range(T):
        p_v[ROWS : ROWS + 1, L * t : L * (t + 1)] = halo_r[t : t + 1, :]

    lax.fori_loop(23, 32, trans, 0)

    own_main.wait()
    for o in range(1, GX):
        main_copy(o).wait()
    sent(2)
    sums = in_main[0]
    for g in range(1, GX):
        sums += in_main[g]
    sums_out[...] = sums


def field(off, x, amp, mats, tw):
    hbm = pl.BlockSpec(memory_space=pltpu.HBM)
    vmem = pl.BlockSpec(memory_space=pltpu.VMEM)
    piece = (PER, 2, 8, L)
    return pl.pallas_call(
        field_kernel,
        out_shape=(
            jax.ShapeDtypeStruct((ROWS, N), F32),
            jax.ShapeDtypeStruct((ROWS, N), F32),
            jax.ShapeDtypeStruct((T, L), F32),
        ),
        in_specs=[hbm] * 5,
        out_specs=(vmem, vmem, vmem),
        scratch_shapes=[
            pltpu.SMEM((2,), jnp.int32),
            pltpu.VMEM(tw.shape, F32),
            pltpu.VMEM(mats.shape, BF16),
            pltpu.VMEM((ROWS + 8, N), F32),
            pltpu.VMEM((SLOTS, ROWS, 2 * L), F32),
            pltpu.VMEM((G, CHUNKS, 2) + piece, F32),
            pltpu.VMEM((CHUNKS, G, 2) + piece, F32),
            pltpu.VMEM((G, 2, CHUNKS) + piece, F32),
            pltpu.VMEM((2, CHUNKS, G) + piece, F32),
            pltpu.VMEM((T, 8 * PER, 2 * L), F32),
            pltpu.VMEM((T, 8, 2 * L), F32),
            pltpu.VMEM((T, 8 * SLOTS, L), F32),
            pltpu.VMEM((2 * L + 16, L), F32),
            pltpu.VMEM((T, L), F32),
            pltpu.VMEM((T, L), F32),
            pltpu.VMEM((2, T * ROWS + 32, L), F32),
            pltpu.VMEM((2, T, T, L), F32),
            pltpu.VMEM((2, T, T, L), F32),
            pltpu.VMEM((2 * T, N), F32),
            pltpu.VMEM((T + 8, L), F32),
            pltpu.VMEM((T + 8, L), F32),
            pltpu.VMEM((GX, T, L), F32),
            pltpu.VMEM((GX, T, L), F32),
            pltpu.VMEM((1024 + L, L), BF16),
            pltpu.SemaphoreType.DMA((8,)),
            pltpu.SemaphoreType.DMA((5,)),
            pltpu.SemaphoreType.DMA((CHUNKS + 1, G)),
            pltpu.SemaphoreType.DMA((CHUNKS + 1, G)),
            pltpu.SemaphoreType.DMA((3, CHUNKS, G)),
            pltpu.SemaphoreType.DMA((3, CHUNKS, G)),
            pltpu.SemaphoreType.DMA((24,)),
        ],
        compiler_params=pltpu.CompilerParams(
            collective_id=0, has_side_effects=True, vmem_limit_bytes=44 << 20
        ),
        name="field",
    )(*(pltpu.with_memory_space_constraint(v, pltpu.HBM) for v in (off, x, amp, mats, tw)))


def write_kernel(tx, ty, sums, tx_out, ty_out, up_out, sem):
    copies = []
    for n, (src, dst) in enumerate(((tx, tx_out), (ty, ty_out))):
        for i in range(4):
            rows = pl.ds(ROWS // 4 * i, ROWS // 4)
            copies.append(pltpu.make_async_copy(src.at[rows], dst.at[rows], sem.at[4 * n + i]))
    for cp in copies:
        cp.start()
    up_out[...] = jnp.sqrt(sums[:, : L // 2] / sums[:, L // 2 :])
    for cp in copies:
        cp.wait()


def written(tx, ty, ratio):
    hbm = pl.BlockSpec(memory_space=pltpu.HBM)
    vmem = pl.BlockSpec(memory_space=pltpu.VMEM)
    return pl.pallas_call(
        write_kernel,
        out_shape=(
            jax.ShapeDtypeStruct((ROWS, N), F32),
            jax.ShapeDtypeStruct((ROWS, N), F32),
            jax.ShapeDtypeStruct((T, L // 2), F32),
        ),
        in_specs=[pl.BlockSpec(memory_space=pl.ANY)] * 2 + [vmem],
        out_specs=(hbm, hbm, vmem),
        scratch_shapes=[pltpu.SemaphoreType.DMA((8,))],
        compiler_params=pltpu.CompilerParams(vmem_limit_bytes=1 << 20),
        name="write",
    )(tx, ty, ratio)


def shards(white_noise, amplitude, offsets):
    mats, tw = tables()
    tx, ty, ratio = field(offsets, white_noise[0], amplitude, jnp.asarray(mats), jnp.asarray(tw))
    trans_x, trans_y, upscaled = written(tx, ty, ratio)
    return trans_x[None], trans_y[None], upscaled


def solution(mesh):
    return jax.shard_map(
        shards,
        mesh=mesh,
        in_specs=(P("gx", "gy", None), P(None, "gy"), P()),
        out_specs=(P("gx", "gy", None), P("gx", "gy", None), P("gy", "gx")),
        check_vma=False,
    )
```
